128 devices in a mesh: seq: 16 (over x_lo, y, core), tp: 8 (over x_hi, z).
Axes of the slice: x: 4 (x_hi: 2, x_lo: 2; x = x_hi * 2 + x_lo), y: 4, z: 4, core: 2. Of those that a mesh axis runs over, the one named last changes fastest.
Arguments:
- embeddings: bfloat16 [6144, 4096], P('seq', 'tp'), may hold values from -6 to 6
- span_mask: int32 [6144], P('seq'), may hold values from 0 to 1, as said below
- sentinel_id: int32 [6144], P('seq'), may hold values from 0 to 99, as said below
- sentinel_table: bfloat16 [100, 4096], P(None, 'tp'), may hold values from -6 to 6
- gen_weight: bfloat16 [4096, 240], P(None, 'tp'), may hold values from -0.1875 to 0.1875
- up_weight: bfloat16 [4096, 8192], P(None, 'tp'), may hold values from -0.09375 to 0.09375
- down_weight: bfloat16 [8192, 4096], P('tp'), may hold values from -0.0625 to 0.0625
- cotangent: bfloat16 [6144, 4096], P('seq', 'tp'), may hold values from -0.59765625 to 0.59765625
Outputs:
- layer_output: bfloat16 [6144, 4096], P('seq', 'tp')
- embed_grad: float32 [6144, 4096], P('seq', 'tp')
- table_grad: float32 [100, 4096], P(None, 'tp')
- gen_grad: float32 [4096, 240], P(None, 'tp')
- up_grad: float32 [4096, 8192], P('seq', 'tp')
- down_grad: float32 [8192, 4096], P('tp', 'seq')
The draws below stay inside these ranges and needn't reach their ends.
Inputs may be any that keep to these rules, and one draw needn't show every extreme that they name: `span_mask`: the tokens fall into aligned blocks of 16; each block holds exactly one span of 1 to 3 consecutive tokens marked 1, the rest 0. `sentinel_id`: all 16 tokens of an aligned block carry the same sentinel id.
All inputs are finite; a program needn't handle non-finite values.
Results may differ from the reference program's by a relative error of at most 0.035.
Values may be sent and summed in bfloat16 or wider, within the bound.
No kernel may reach another device: no remote copies, remote signals or barrier semaphores. Data moves between devices by JAX's collectives and lax.ppermute only.
A program may use at most 192 MiB of HBM per device.

```python
import jax
import jax.numpy as jnp
from jax import lax

D = 4096
FF = 8192
HEADS = 16
KW = 15
SENT = 100
TOK_DEV = 384
LENGTH = 6144
N_SEQ = 16
N_TP = 8


def span_layout(key):
    blocks = LENGTH // 16
    key_start, key_length, key_ids, key_top = jax.random.split(jax.random.fold_in(key, 11), 4)
    span_start = jax.random.randint(key_start, (blocks,), 0, 14)
    span_length = jax.random.randint(key_length, (blocks,), 1, 4)
    block_ids = jax.random.randint(key_ids, (blocks,), 0, SENT)
    top_block = jax.random.randint(key_top, (), 0, blocks)
    block_ids = jnp.where(jnp.arange(blocks) == top_block, SENT - 1, block_ids)
    offset = jnp.arange(16)[None, :]
    inside = (offset >= span_start[:, None]) & (offset < span_start[:, None] + span_length[:, None])
    span_mask = inside.astype(jnp.int32).reshape(-1)
    sentinel = jnp.broadcast_to(block_ids[:, None], (blocks, 16)).reshape(-1).astype(jnp.int32)
    return (span_mask, sentinel)


def draw_span_mask(key, part):
    return span_layout(key)[0]


def draw_sentinel_id(key, part):
    return span_layout(key)[1]


def raised(array, stream_key, source, target, parts, factor):
    def block_of(axis_at):
        return (jnp.arange(array.shape[axis_at]) // (array.shape[axis_at] // parts)).reshape((-1,) + (1,) * (array.ndim - 1 - axis_at))

    near = jax.random.permutation(stream_key, parts)[block_of(target)]
    other_side = (block_of(target) + parts // 2) % parts
    return jnp.where((block_of(source) == near) | (block_of(source) == other_side), factor * array, array)


def shard_levels(rng, shape, shards, smallest, high):
    level, own = 1.0, jax.random.fold_in(rng, 6)
    for axis_at, shards_of in shards:
        heights = jnp.exp(jax.random.uniform(jax.random.fold_in(own, axis_at), (shards_of,), jnp.float32, smallest / len(shards), high / len(shards)))
        level = level * jnp.repeat(heights, shape[axis_at] // shards_of).reshape([-1 if axis == axis_at else 1 for axis in range(len(shape))])
    return level


def noise(own_key, dims, scale, limit, cuts=(), kind=jnp.bfloat16):
    loudness = shard_levels(own_key, dims, cuts, -0.22, 0.18) if cuts else 1.0
    result = jax.random.normal(own_key, dims, jnp.float32) * scale * loudness
    return jnp.minimum(jnp.maximum(result, -limit), limit).astype(kind)


def bell_draw_with(key, dims, deviation, reach, shards, heavy, held_as=jnp.bfloat16):
    result = deviation * jax.random.normal(key, dims, jnp.float32)
    if shards:
        result = result * shard_levels(key, dims, shards, -0.22, 0.18)
    return jnp.clip(raised(result, jax.random.fold_in(key, 3), *heavy), -reach, reach).astype(held_as)


def setup_inputs(seed: int = 0) -> dict:
    key_of = jax.random.split(jax.random.key(seed), 9)
    return {
        "embeddings": noise(key_of[0], (LENGTH, D), 1.0, 6.0, ((0, 16), (1, 8))),
        "span_mask": draw_span_mask(jax.random.fold_in(key_of[8], 71), 0),
        "sentinel_id": draw_sentinel_id(jax.random.fold_in(key_of[8], 71), 0),
        "sentinel_table": noise(key_of[3], (SENT, D), 1.0, 6.0, ((1, 8),)),
        "gen_weight": noise(key_of[4], (D, HEADS * KW), (D // 4) ** -0.5, 0.1875, ((1, 8),)),
        "up_weight": noise(key_of[5], (D, FF), D ** -0.5, 0.09375, ((1, 8),)),
        "down_weight": noise(key_of[6], (FF, D), FF ** -0.5, 0.0625, ((0, 8),)),
        "cotangent": bell_draw_with(key_of[7], (LENGTH, D), 0.1, 0.59765625, ((0, 16), (1, 8)), (0, 1, 16, 2.0)),
    }


def gelu_tanh(values):
    return jax.nn.gelu(values, approximate=True)

def rounded(values):
    return lax.optimization_barrier(values.astype(jnp.bfloat16)).astype(jnp.float32)

def reference(embeddings, span_mask, sentinel_id, sentinel_table, gen_weight, up_weight, down_weight, cotangent):
    tap_reach = (KW - 1) // 2
    head_width = D // HEADS
    onehot = sentinel_id[:, None] == jnp.arange(SENT, dtype=jnp.int32)[None, :]
    picked = jnp.dot(onehot.astype(jnp.bfloat16), sentinel_table, preferred_element_type=jnp.float32).astype(jnp.bfloat16)
    masked = span_mask[:, None] == 1
    hidden = jnp.where(masked, picked, embeddings)
    logits = jnp.dot(hidden, gen_weight, preferred_element_type=jnp.float32)
    exp_logits = jnp.exp(logits.reshape(LENGTH, HEADS, KW))
    kernel = exp_logits / lax.optimization_barrier(jnp.sum(exp_logits, axis=-1, keepdims=True))
    padded = jnp.pad(hidden, ((tap_reach, tap_reach), (0, 0))).reshape(LENGTH + 2 * tap_reach, HEADS, head_width).astype(jnp.float32)
    conv_sum = jnp.zeros((LENGTH, HEADS, head_width), jnp.float32)
    for tap_index in range(KW):
        conv_sum = conv_sum + kernel[:, :, tap_index, None] * padded[tap_index:tap_index + LENGTH]
    act = (hidden.astype(jnp.float32) + conv_sum.reshape(LENGTH, D)).astype(jnp.bfloat16)
    pre_act = jnp.dot(act, up_weight, preferred_element_type=jnp.float32)
    middle, gelu_back = jax.vjp(gelu_tanh, pre_act)
    middle = middle.astype(jnp.bfloat16)
    block_size = FF // N_TP
    ffn_total = jnp.zeros((LENGTH, D), jnp.float32)
    for group_index in range(N_TP):
        lower = group_index * block_size
        ffn_total = ffn_total + rounded(jnp.dot(middle[:, lower:lower + block_size], down_weight[lower:lower + block_size], preferred_element_type=jnp.float32))
    layer_output = (act.astype(jnp.float32) + ffn_total).astype(jnp.bfloat16)
    middle_grad = jnp.dot(cotangent, down_weight.T, preferred_element_type=jnp.float32)
    pre_grad = gelu_back(middle_grad)[0].astype(jnp.bfloat16)
    down_grad = jnp.zeros((FF, D), jnp.float32)
    up_grad = jnp.zeros((D, FF), jnp.float32)
    for group_index in range(N_SEQ):
        lower = group_index * TOK_DEV
        down_grad = down_grad + rounded(jnp.dot(middle[lower:lower + TOK_DEV].T, cotangent[lower:lower + TOK_DEV], preferred_element_type=jnp.float32))
        up_grad = up_grad + rounded(jnp.dot(act[lower:lower + TOK_DEV].T, pre_grad[lower:lower + TOK_DEV], preferred_element_type=jnp.float32))
    act_grad = cotangent.astype(jnp.float32)
    for group_index in range(N_TP):
        lower = group_index * block_size
        act_grad = act_grad + rounded(jnp.dot(pre_grad[:, lower:lower + block_size], up_weight[:, lower:lower + block_size].T, preferred_element_type=jnp.float32))
    act_three = act_grad.reshape(LENGTH, HEADS, head_width)
    kernel_grad = jnp.stack([lax.optimization_barrier(jnp.sum(act_three * padded[tap_index:tap_index + LENGTH], axis=-1)) for tap_index in range(KW)], axis=-1)
    weighted = lax.optimization_barrier(jnp.sum(kernel * kernel_grad, axis=-1, keepdims=True))
    logit_grad = (kernel * (kernel_grad - weighted)).reshape(LENGTH, HEADS * KW).astype(jnp.bfloat16)
    gen_grad = jnp.dot(hidden.T, logit_grad, preferred_element_type=jnp.float32)
    grad_pad = jnp.pad(act_three, ((tap_reach, tap_reach), (0, 0), (0, 0)))
    kernel_pad = jnp.pad(kernel, ((tap_reach, tap_reach), (0, 0), (0, 0)))
    conv_back = jnp.zeros((LENGTH, HEADS, head_width), jnp.float32)
    for tap_index in range(KW):
        lower = 2 * tap_reach - tap_index
        conv_back = conv_back + kernel_pad[lower:lower + LENGTH, :, tap_index, None] * grad_pad[lower:lower + LENGTH]
    hidden_grad = act_grad + conv_back.reshape(LENGTH, D) + jnp.dot(logit_grad, gen_weight.T, preferred_element_type=jnp.float32)
    embed_grad = jnp.where(masked, jnp.float32(0.0), hidden_grad)
    table_grad = jnp.dot(onehot.astype(jnp.float32).T, jnp.where(masked, hidden_grad, jnp.float32(0.0)), precision=lax.Precision.HIGHEST)
    return (layer_output, embed_grad, table_grad, gen_grad, up_grad, down_grad)
```

```python
import functools

import jax
import jax.numpy as jnp
from jax import lax
from jax.experimental import pallas as pl
from jax.experimental.pallas import tpu as pltpu
from jax.sharding import PartitionSpec as P

KW = 15
REACH = 7
PAD = 8
ROWS = 32
F32 = jnp.float32
BF16 = jnp.bfloat16
NT = (((1,), (1,)), ((), ()))
TN = (((0,), (0,)), ((), ()))


def params(megabytes):
    return pltpu.CompilerParams(vmem_limit_bytes=megabytes << 20)


def flip(value, axis, bit):
    count = lax.axis_size(axis)
    return lax.ppermute(value, axis, [(i, i ^ bit) for i in range(count)])


def halo(value):
    count = lax.axis_size("seq")
    forward = [(i, i + 1) for i in range(count - 1)]
    backward = [(i + 1, i) for i in range(count - 1)]
    low = lax.ppermute(value[-PAD:], "seq", forward)
    high = lax.ppermute(value[:PAD], "seq", backward)
    return low, high


def exchange(blocks):
    shape = blocks.shape
    cube = blocks.reshape((2, 2, 2) + shape[1:])
    for place, bit in enumerate((4, 2, 1)):
        keep = lax.index_in_dim(cube, 0, place, keepdims=True)
        send = lax.index_in_dim(cube, 1, place, keepdims=True)
        cube = jnp.concatenate([keep, flip(send, "tp", bit)], axis=place)
    return cube.reshape(shape)


def reduce_blocks(blocks):
    half = blocks.shape[0] // 2
    while half:
        blocks = blocks[:half] + flip(blocks[half:], "tp", half)
        half //= 2
    return blocks[0]


def gather_small(value):
    blocks = value[None]
    for bit in (1, 2, 4):
        blocks = jnp.concatenate([blocks, flip(blocks, "tp", bit)], axis=0)
    return blocks


def sum_over_seq(value):
    for bit in (1, 2, 4, 8):
        sent = value.astype(BF16)
        value = sent.astype(F32) + flip(sent, "seq", bit).astype(F32)
    return value


def gather_pieces(value):
    half = value.shape[0] // 2
    four = flip(value, "tp", 4)
    one = flip(value, "tp", 1)
    three = flip(value, "tp", 3)
    five = flip(four, "tp", 1)
    seven = flip(four, "tp", 3)
    two_a = flip(one[:half], "tp", 3)
    two_b = flip(three[half:], "tp", 1)
    six_a = flip(five[:half], "tp", 3)
    six_b = flip(seven[half:], "tp", 1)
    return value, one, three, four, five, seven, two_a, two_b, six_a, six_b


def conv_forward_kernel(logit_ref, hidden_ref, low_ref, high_ref, act_ref, tap_ref, padded):
    rows = hidden_ref.shape[0]
    width = hidden_ref.shape[1]
    heads = 2
    exps = jnp.exp(logit_ref[...])
    first = exps[0:KW]
    second = exps[KW : 2 * KW]
    first = first / jnp.sum(first, axis=0, keepdims=True)
    second = second / jnp.sum(second, axis=0, keepdims=True)
    blank = jnp.zeros((ROWS - 2 * KW, rows), F32)
    tap_ref[...] = jnp.concatenate([first, second, blank], axis=0).T
    padded[0:PAD] = low_ref[...].astype(F32)
    padded[PAD : PAD + rows] = hidden_ref[...].astype(F32)
    padded[PAD + rows :] = high_ref[...].astype(F32)
    step = 32
    head_width = width // heads

    def run(index, carry):
        base = pl.multiple_of(index * step, step)
        taps = tap_ref[pl.ds(base, step), :]
        for head in range(heads):
            lanes = slice(head * head_width, (head + 1) * head_width)
            window = padded[pl.ds(base, step + 2 * PAD), lanes]
            total = jnp.zeros((step, head_width), F32)
            for tap in range(KW):
                column = head * KW + tap
                total = total + taps[:, column : column + 1] * window[tap + 1 : tap + 1 + step]
            act_ref[pl.ds(base, step), lanes] = (window[PAD : PAD + step] + total).astype(BF16)
        return carry

    lax.fori_loop(0, rows // step, run, 0)


def conv_forward(logits, hidden, low, high):
    rows, width = hidden.shape
    return pl.pallas_call(
        conv_forward_kernel,
        out_shape=(
            jax.ShapeDtypeStruct((rows, width), BF16),
            jax.ShapeDtypeStruct((rows, ROWS), F32),
        ),
        scratch_shapes=[pltpu.VMEM((rows + 2 * PAD, width), F32)],
        name="conv_forward",
    )(logits, hidden, low, high)


def grad_middle_kernel(cot_ref, down_ref, out_ref):
    width = cot_ref.shape[2]
    total = jnp.zeros(out_ref.shape, F32)
    for piece in range(cot_ref.shape[0]):
        total = total + lax.dot_general(
            cot_ref[piece],
            down_ref[:, piece * width : (piece + 1) * width],
            NT,
            preferred_element_type=F32,
        )
    out_ref[...] = total


def grad_middle(cot_full, down_weight):
    pieces, rows, width = cot_full.shape
    units = down_weight.shape[0]
    block = 256
    return pl.pallas_call(
        grad_middle_kernel,
        grid=(units // block,),
        in_specs=[
            pl.BlockSpec((pieces, rows, width), lambda i: (0, 0, 0)),
            pl.BlockSpec((block, pieces * width), lambda i: (i, 0)),
        ],
        out_specs=pl.BlockSpec((rows, block), lambda i: (0, i)),
        out_shape=jax.ShapeDtypeStruct((rows, units), F32),
        compiler_params=params(40),
        name="grad_middle",
    )(cot_full, down_weight)


def up_kernel(order, *refs):
    pieces = refs[:10]
    up_ref, grad_ref, full_ref, middle_ref, pre_grad_ref = refs[10:]
    half = full_ref.shape[1] // 2
    width = full_ref.shape[2]

    @pl.when(pl.program_id(0) == 0)
    def _():
        for at, ref in zip((0, 1, 3, 4, 5, 7), pieces[:6]):
            full_ref[order[at]] = ref[...]
        full_ref[order[2], 0:half] = pieces[6][...]
        full_ref[order[2], half:] = pieces[7][...]
        full_ref[order[6], 0:half] = pieces[8][...]
        full_ref[order[6], half:] = pieces[9][...]

    pre = jnp.zeros(middle_ref.shape, F32)
    for piece in range(full_ref.shape[0]):
        pre = pre + jnp.dot(
            full_ref[piece],
            up_ref[piece * width : (piece + 1) * width, :],
            preferred_element_type=F32,
        )
    scale = 0.7978845608028654
    square = pre * pre
    bent = jnp.tanh(scale * (pre + 0.044715 * (square * pre)))
    middle_ref[...] = (0.5 * pre * (1.0 + bent)).astype(BF16)
    slope = 0.5 * (1.0 + bent) + 0.5 * pre * (1.0 - bent * bent) * (
        scale * (1.0 + 3.0 * 0.044715 * square)
    )
    pre_grad_ref[...] = (grad_ref[...] * slope).astype(BF16)


def up_project(order, pieces, up_weight, middle_grad):
    rows, width = pieces[0].shape
    depth, units = up_weight.shape
    block = 256
    whole = [pl.BlockSpec(p.shape, lambda i, o: (0, 0)) for p in pieces]
    return pl.pallas_call(
        up_kernel,
        grid_spec=pltpu.PrefetchScalarGridSpec(
            num_scalar_prefetch=1,
            grid=(units // block,),
            in_specs=whole
            + [
                pl.BlockSpec((depth, block), lambda i, o: (0, i)),
                pl.BlockSpec((rows, block), lambda i, o: (0, i)),
            ],
            out_specs=[
                pl.BlockSpec((depth // width, rows, width), lambda i, o: (0, 0, 0)),
                pl.BlockSpec((rows, block), lambda i, o: (0, i)),
                pl.BlockSpec((rows, block), lambda i, o: (0, i)),
            ],
        ),
        out_shape=(
            jax.ShapeDtypeStruct((depth // width, rows, width), BF16),
            jax.ShapeDtypeStruct((rows, units), BF16),
            jax.ShapeDtypeStruct((rows, units), BF16),
        ),
        compiler_params=params(48),
        name="up_project",
    )(order, *pieces, up_weight, middle_grad)


def spread_kernel(dims, order, value_ref, weight_ref, *out_refs):
    result = lax.dot_general(
        value_ref[...], weight_ref[...], dims, preferred_element_type=F32
    ).astype(BF16)
    for index, ref in enumerate(out_refs):

        @pl.when(pl.program_id(0) == index)
        def _(ref=ref):
            ref[...] = result


def spread(order, value, weight, transposed, name):
    rows, units = value.shape
    if transposed:
        width = weight.shape[0] // 8
        spec = pl.BlockSpec((width, units), lambda k, o: (o[k], 0))
        dims = NT
    else:
        width = weight.shape[1] // 8
        spec = pl.BlockSpec((units, width), lambda k, o: (0, o[k]))
        dims = (((1,), (0,)), ((), ()))
    return pl.pallas_call(
        functools.partial(spread_kernel, dims),
        grid_spec=pltpu.PrefetchScalarGridSpec(
            num_scalar_prefetch=1,
            grid=(8,),
            in_specs=[pl.BlockSpec((rows, units), lambda k, o: (0, 0)), spec],
            out_specs=[pl.BlockSpec((rows, width), lambda k, o: (0, 0))] * 8,
        ),
        out_shape=[jax.ShapeDtypeStruct((rows, width), BF16)] * 8,
        compiler_params=params(40),
        name=name,
    )(order, value, weight)


def weight_grads_kernel(act_ref, cot_ref, pre_grad_ref, middle_ref, out_ref):
    up = lax.dot_general(act_ref[0], pre_grad_ref[...], TN, preferred_element_type=F32)
    down = lax.dot_general(cot_ref[0], middle_ref[...], TN, preferred_element_type=F32)
    chunk = out_ref.shape[1] // 2
    for index in range(out_ref.shape[0]):
        rows = slice(index * chunk, (index + 1) * chunk)
        out_ref[index, 0:chunk] = up[rows].astype(BF16)
        out_ref[index, chunk:] = down[rows].astype(BF16)


def weight_grads(act_full, cot_full, pre_grad, middle):
    pieces, rows, width = act_full.shape
    units = middle.shape[1]
    chunks = lax.axis_size("seq")
    per = chunks // pieces
    chunk = width // per
    return pl.pallas_call(
        weight_grads_kernel,
        grid=(pieces,),
        in_specs=[
            pl.BlockSpec((1, rows, width), lambda i: (i, 0, 0)),
            pl.BlockSpec((1, rows, width), lambda i: (i, 0, 0)),
            pl.BlockSpec((rows, units), lambda i: (0, 0)),
            pl.BlockSpec((rows, units), lambda i: (0, 0)),
        ],
        out_specs=pl.BlockSpec((per, 2 * chunk, units), lambda i: (i, 0, 0)),
        out_shape=jax.ShapeDtypeStruct((chunks, 2 * chunk, units), BF16),
        compiler_params=params(40),
        name="weight_grads",
    )(act_full, cot_full, pre_grad, middle)


def kernel_grad_kernel(*refs):
    terms = refs[:8]
    cot_ref, hidden_ref, low_ref, high_ref, tap_ref, grad_ref, logit_ref, padded = refs[8:]
    rows, width = hidden_ref.shape
    heads = 2
    head_width = width // heads
    padded[0:PAD] = low_ref[...].astype(F32)
    padded[PAD : PAD + rows] = hidden_ref[...].astype(F32)
    padded[PAD + rows :] = high_ref[...].astype(F32)
    step = 32
    lane = lax.broadcasted_iota(jnp.int32, (step, ROWS), 1)

    def run(index, carry):
        base = pl.multiple_of(index * step, step)
        at = pl.ds(base, step)
        grad = terms[0][at, :].astype(F32)
        for ref in terms[1:]:
            grad = grad + ref[at, :].astype(F32)
        grad = grad + cot_ref[at, :].astype(F32)
        grad_ref[at, :] = grad
        taps = tap_ref[at, :]
        found = jnp.zeros((step, ROWS), F32)
        for head in range(heads):
            lanes = slice(head * head_width, (head + 1) * head_width)
            window = padded[pl.ds(base, step + 2 * PAD), lanes]
            part = grad[:, lanes]
            for tap in range(KW):
                column = head * KW + tap
                value = jnp.sum(part * window[tap + 1 : tap + 1 + step], axis=1, keepdims=True)
                found = jnp.where(lane == column, value, found)
        product = taps * found
        in_first = lane < KW
        one = jnp.sum(jnp.where(in_first, product, 0.0), axis=1, keepdims=True)
        two = jnp.sum(jnp.where(in_first, 0.0, product), axis=1, keepdims=True)
        logit_ref[at, :] = taps * (found - jnp.where(in_first, one, two))
        return carry

    lax.fori_loop(0, rows // step, run, 0)


def kernel_grads(terms, cotangent, hidden, low, high, taps):
    rows, width = hidden.shape
    return pl.pallas_call(
        kernel_grad_kernel,
        out_shape=(
            jax.ShapeDtypeStruct((rows, width), F32),
            jax.ShapeDtypeStruct((rows, ROWS), F32),
        ),
        scratch_shapes=[pltpu.VMEM((rows + 2 * PAD, width), F32)],
        compiler_params=params(32),
        name="kernel_grads",
    )(*terms, cotangent, hidden, low, high, taps)


def hidden_grad_kernel(
    grad_ref,
    glow_ref,
    ghigh_ref,
    tap_ref,
    tlow_ref,
    thigh_ref,
    logit_ref,
    gen_ref,
    mask_ref,
    code_ref,
    embed_ref,
    table_ref,
    padded,
    tapped,
    back,
):
    rows, width = grad_ref.shape
    heads = 2
    head_width = width // heads
    padded[0:PAD] = glow_ref[...].astype(F32)
    padded[PAD : PAD + rows] = grad_ref[...]
    padded[PAD + rows :] = ghigh_ref[...].astype(F32)
    tapped[0:PAD] = tlow_ref[...]
    tapped[PAD : PAD + rows] = tap_ref[...]
    tapped[PAD + rows :] = thigh_ref[...]
    back[...] = lax.dot_general(logit_ref[...], gen_ref[...], TN, preferred_element_type=F32)
    step = 32

    def run(index, carry):
        base = pl.multiple_of(index * step, step)
        at = pl.ds(base, step)
        picked = mask_ref[at, :] == 1
        taps = tapped[pl.ds(base, step + 2 * PAD), :]
        for head in range(heads):
            lanes = slice(head * head_width, (head + 1) * head_width)
            window = padded[pl.ds(base, step + 2 * PAD), lanes]
            total = window[PAD : PAD + step] + back[at, lanes]
            for tap in range(KW):
                column = head * KW + tap
                lower = 2 * PAD - 1 - tap
                total = (
                    total
                    + taps[lower : lower + step, column : column + 1]
                    * window[lower : lower + step]
                )
            embed_ref[at, lanes] = jnp.where(picked, 0.0, total)
            back[at, lanes] = jnp.where(picked, total, 0.0)
        return carry

    lax.fori_loop(0, rows // step, run, 0)
    codes = lax.broadcasted_iota(jnp.int32, (table_ref.shape[0], rows), 0)
    chosen = jnp.where(codes == code_ref[...], 1.0, 0.0).astype(BF16)
    value = back[...]
    upper = value.astype(BF16)
    lower = (value - upper.astype(F32)).astype(BF16)
    table_ref[...] = jnp.dot(chosen, upper, preferred_element_type=F32) + jnp.dot(
        chosen, lower, preferred_element_type=F32
    )


def hidden_grads(grad, glow, ghigh, taps, tlow, thigh, logit_full, gen_full, mask, code, codes):
    rows, width = grad.shape
    return pl.pallas_call(
        hidden_grad_kernel,
        out_shape=(
            jax.ShapeDtypeStruct((rows, width), F32),
            jax.ShapeDtypeStruct((codes, width), F32),
        ),
        scratch_shapes=[
            pltpu.VMEM((rows + 2 * PAD, width), F32),
            pltpu.VMEM((rows + 2 * PAD, ROWS), F32),
            pltpu.VMEM((rows, width), F32),
        ],
        compiler_params=params(32),
        name="hidden_grads",
    )(grad, glow, ghigh, taps, tlow, thigh, logit_full, gen_full, mask, code)


def place_kernel(order, blocks_ref, out_ref):
    width = blocks_ref.shape[2]
    for piece in range(blocks_ref.shape[0]):
        at = pl.multiple_of(order[piece] * width, width)
        out_ref[:, pl.ds(at, width)] = blocks_ref[piece, 0 : out_ref.shape[0]]


def place(order, blocks, rows):
    pieces, _, width = blocks.shape
    return pl.pallas_call(
        place_kernel,
        grid_spec=pltpu.PrefetchScalarGridSpec(
            num_scalar_prefetch=1,
            grid=(1,),
            in_specs=[pl.BlockSpec(blocks.shape, lambda i, o: (0, 0, 0))],
            out_specs=pl.BlockSpec((rows, pieces * width), lambda i, o: (0, 0)),
        ),
        out_shape=jax.ShapeDtypeStruct((rows, pieces * width), F32),
        name="place",
    )(order, blocks)


def body(
    embeddings,
    span_mask,
    sentinel_id,
    sentinel_table,
    gen_weight,
    up_weight,
    down_weight,
    cotangent,
):
    rows, width = embeddings.shape
    codes = sentinel_table.shape[0]
    members = lax.axis_size("tp")
    me = lax.axis_index("tp")
    order = jnp.arange(members, dtype=jnp.int32) ^ me.astype(jnp.int32)

    columns = gen_weight.shape[1]
    gen_rows = jnp.pad(gen_weight.T, ((0, ROWS - columns), (0, 0)))
    gen_own = jnp.stack(
        [
            lax.dynamic_slice(gen_rows, (jnp.int32(0), order[k] * width), (ROWS, width))
            for k in range(members)
        ]
    )
    gen_full = exchange(gen_own).reshape(members * ROWS, width)
    cot_full = lax.all_gather(cotangent, "tp", axis=0, tiled=False)

    sentinel_codes = jnp.arange(codes, dtype=jnp.int32)
    onehot = (sentinel_id[:, None] == sentinel_codes[None, :]).astype(BF16)
    picked = jnp.dot(onehot, sentinel_table, preferred_element_type=F32).astype(BF16)
    hidden = jnp.where(span_mask[:, None] == 1, picked, embeddings)
    low, high = halo(hidden)

    logit_part = lax.dot_general(gen_full, hidden, NT, preferred_element_type=F32)
    logits = reduce_blocks(logit_part.reshape(members, ROWS, rows))
    act, taps = conv_forward(logits, hidden, low, high)
    tap_low, tap_high = halo(taps)

    pieces = gather_pieces(act)
    middle_grad = grad_middle(cot_full, down_weight)
    act_full, middle, pre_grad = up_project(order, pieces, up_weight, middle_grad)

    back_terms = spread(order, pre_grad, up_weight, True, "act_back")
    back_terms = [back_terms[0]] + [flip(back_terms[k], "tp", k) for k in range(1, members)]
    summed = weight_grads(act_full, cot_full, pre_grad, middle)
    summed = lax.psum_scatter(summed, "seq", scatter_dimension=0, tiled=False)

    grad, logit_grad = kernel_grads(back_terms, cotangent, hidden, low, high, taps)
    grad_low, grad_high = halo(grad.astype(BF16))
    logit_full = gather_small(logit_grad.astype(BF16).T)
    logit_full = logit_full.reshape(members * ROWS, rows)
    embed_grad, table_part = hidden_grads(
        grad,
        grad_low,
        grad_high,
        taps,
        tap_low,
        tap_high,
        logit_full,
        gen_full,
        span_mask[:, None],
        sentinel_id[None, :],
        codes,
    )
    gen_part = jnp.dot(logit_full, hidden, preferred_element_type=F32).astype(BF16)
    gen_part = exchange(gen_part.reshape(members, ROWS, width)).astype(F32)
    gen_sum = sum_over_seq(gen_part)
    table_grad = sum_over_seq(table_part)
    gen_grad = place(order, gen_sum, columns).T

    terms = spread(order, middle, down_weight, False, "ffn_out")
    total = terms[0].astype(F32)
    for k in range(1, members):
        total = total + flip(terms[k], "tp", k).astype(F32)
    layer_output = (act.astype(F32) + total).astype(BF16)

    chunk = summed.shape[0] // 2
    up_grad = summed[:chunk].astype(F32)
    down_grad = summed[chunk:].astype(F32).T
    return (layer_output, embed_grad, table_grad, gen_grad, up_grad, down_grad)


def solution(mesh):
    placed = (
        P("seq", "tp"),
        P("seq"),
        P("seq"),
        P(None, "tp"),
        P(None, "tp"),
        P(None, "tp"),
        P("tp", None),
        P("seq", "tp"),
    )
    return jax.shard_map(
        body,
        mesh=mesh,
        in_specs=placed,
        out_specs=(
            P("seq", "tp"),
            P("seq", "tp"),
            P(None, "tp"),
            P(None, "tp"),
            P("seq", "tp"),
            P("tp", "seq"),
        ),
        check_vma=False,
    )
```

```python
import functools

import jax
import jax.numpy as jnp
from jax import lax
from jax.experimental import pallas as pl
from jax.experimental.pallas import tpu as pltpu
from jax.sharding import PartitionSpec as P

KW = 15
REACH = 7
PAD = 8
ROWS = 32
F32 = jnp.float32
BF16 = jnp.bfloat16
NT = (((1,), (1,)), ((), ()))
TN = (((0,), (0,)), ((), ()))


def params(megabytes):
    return pltpu.CompilerParams(vmem_limit_bytes=megabytes << 20)


def flip(value, axis, bit):
    count = lax.axis_size(axis)
    return lax.ppermute(value, axis, [(i, i ^ bit) for i in range(count)])


def halo(value):
    count = lax.axis_size("seq")
    forward = [(i, i + 1) for i in range(count - 1)]
    backward = [(i + 1, i) for i in range(count - 1)]
    low = lax.ppermute(value[-PAD:], "seq", forward)
    high = lax.ppermute(value[:PAD], "seq", backward)
    return low, high


def exchange(blocks):
    shape = blocks.shape
    cube = blocks.reshape((2, 2, 2) + shape[1:])
    for place, bit in enumerate((4, 2, 1)):
        keep = lax.index_in_dim(cube, 0, place, keepdims=True)
        send = lax.index_in_dim(cube, 1, place, keepdims=True)
        cube = jnp.concatenate([keep, flip(send, "tp", bit)], axis=place)
    return cube.reshape(shape)


def gather_small(value):
    blocks = value[None]
    for bit in (1, 2, 4):
        blocks = jnp.concatenate([blocks, flip(blocks, "tp", bit)], axis=0)
    return blocks


def sum_over_seq(value):
    for bit in (1, 2, 4, 8):
        sent = value.astype(BF16)
        value = sent.astype(F32) + flip(sent, "seq", bit).astype(F32)
    return value


def gather_pieces(value):
    half = value.shape[0] // 2
    four = flip(value, "tp", 4)
    one = flip(value, "tp", 1)
    three = flip(value, "tp", 3)
    five = flip(four, "tp", 1)
    seven = flip(four, "tp", 3)
    two_a = flip(one[:half], "tp", 3)
    two_b = flip(three[half:], "tp", 1)
    six_a = flip(five[:half], "tp", 3)
    six_b = flip(seven[half:], "tp", 1)
    return value, one, three, four, five, seven, two_a, two_b, six_a, six_b


def hidden_logits_kernel(order, *refs):
    pieces = refs[:10]
    gen_ref, full_ref, edge_ref, flat_ref, tap_ref = refs[10:]
    members, rows, width = full_ref.shape
    half = rows // 2
    for at, ref in zip((0, 1, 3, 4, 5, 7), pieces[:6]):
        full_ref[order[at]] = ref[...]
    full_ref[order[2], 0:half] = pieces[6][...]
    full_ref[order[2], half:] = pieces[7][...]
    full_ref[order[6], 0:half] = pieces[8][...]
    full_ref[order[6], half:] = pieces[9][...]
    logits = jnp.zeros((gen_ref.shape[0], rows), F32)
    for piece in range(members):
        edge_ref[0, piece] = full_ref[piece, 0:PAD]
        edge_ref[1, piece] = full_ref[piece, rows - PAD :]
        logits = logits + lax.dot_general(
            gen_ref[:, piece * width : (piece + 1) * width],
            full_ref[piece],
            NT,
            preferred_element_type=F32,
        )
    exps = jnp.exp(logits)
    first = exps[0:KW]
    second = exps[KW : 2 * KW]
    first = first / jnp.sum(first, axis=0, keepdims=True)
    second = second / jnp.sum(second, axis=0, keepdims=True)
    blank = jnp.zeros((ROWS - 2 * KW, rows), F32)
    flat = jnp.concatenate([first, second, blank], axis=0)
    flat_ref[...] = flat
    tap_ref[...] = flat.T


def hidden_logits(order, pieces, gen_rows):
    rows, width = pieces[0].shape
    columns, depth = gen_rows.shape
    members = depth // width
    whole = [pl.BlockSpec(p.shape, lambda i, o: (0, 0)) for p in pieces]
    return pl.pallas_call(
        hidden_logits_kernel,
        grid_spec=pltpu.PrefetchScalarGridSpec(
            num_scalar_prefetch=1,
            grid=(1,),
            in_specs=whole + [pl.BlockSpec((columns, depth), lambda i, o: (0, 0))],
            out_specs=[
                pl.BlockSpec((members, rows, width), lambda i, o: (0, 0, 0)),
                pl.BlockSpec((2, members, PAD, width), lambda i, o: (0, 0, 0, 0)),
                pl.BlockSpec((ROWS, rows), lambda i, o: (0, 0)),
                pl.BlockSpec((rows, ROWS), lambda i, o: (0, 0)),
            ],
        ),
        out_shape=(
            jax.ShapeDtypeStruct((members, rows, width), BF16),
            jax.ShapeDtypeStruct((2, members, PAD, width), BF16),
            jax.ShapeDtypeStruct((ROWS, rows), F32),
            jax.ShapeDtypeStruct((rows, ROWS), F32),
        ),
        compiler_params=params(32),
        name="hidden_logits",
    )(order, *pieces, gen_rows)


def conv_up_kernel(
    order,
    hidden_ref,
    low_ref,
    high_ref,
    flat_ref,
    up_ref,
    grad_ref,
    act_ref,
    middle_ref,
    pre_grad_ref,
    padded,
    pre,
):
    _, rows, width = hidden_ref.shape
    step = 64
    reach = 2 * step
    heads = 2
    head_width = width // heads
    padded[0:PAD] = low_ref[0]
    padded[PAD : PAD + rows] = hidden_ref[0]
    padded[PAD + rows : 2 * PAD + rows] = high_ref[0]
    padded[2 * PAD + rows :] = jnp.zeros((padded.shape[0] - 2 * PAD - rows, width), BF16)
    flat = flat_ref[0]
    taps = jnp.concatenate([flat, jnp.zeros((reach - ROWS, rows), F32)], axis=0).T
    lane = lax.broadcasted_iota(jnp.int32, (step, reach), 1)
    for base in range(0, rows, step):
        for head in range(heads):
            lanes = slice(head * head_width, (head + 1) * head_width)
            mine = (lane >= head * KW) & (lane < (head + 1) * KW)
            own = jnp.where(mine, taps[base : base + step], 0.0)
            own = pltpu.roll(own, (1 - head * KW) % reach, 1)
            band = pltpu.roll(own, 0, 1, stride=1, stride_axis=0)
            upper = band.astype(BF16)
            lower = (band - upper.astype(F32)).astype(BF16)
            window = padded[base : base + reach, lanes]
            total = jnp.dot(upper, window, preferred_element_type=F32) + jnp.dot(
                lower, window, preferred_element_type=F32
            )
            value = hidden_ref[0, base : base + step, lanes].astype(F32) + total
            act_ref[0, base : base + step, lanes] = value.astype(BF16)
    term = jnp.dot(act_ref[0], up_ref[...], preferred_element_type=F32)

    @pl.when(pl.program_id(0) == 0)
    def _():
        pre[...] = term

    @pl.when(pl.program_id(0) > 0)
    def _():
        pre[...] += term

    @pl.when(pl.program_id(0) == pl.num_programs(0) - 1)
    def _():
        scale = 0.7978845608028654
        chunk = 64

        def run(index, carry):
            at = pl.ds(pl.multiple_of(index * chunk, chunk), chunk)
            value = pre[at, :]
            square = value * value
            bent = jnp.tanh(scale * (value + 0.044715 * (square * value)))
            middle_ref[at, :] = (0.5 * value * (1.0 + bent)).astype(BF16)
            slope = 0.5 * (1.0 + bent) + 0.5 * value * (1.0 - bent * bent) * (
                scale * (1.0 + 3.0 * 0.044715 * square)
            )
            pre_grad_ref[at, :] = (grad_ref[at, :] * slope).astype(BF16)
            return carry

        lax.fori_loop(0, rows // chunk, run, 0)


def conv_up(order, hidden_full, low, high, flat_full, up_weight, middle_grad):
    members, rows, width = hidden_full.shape
    units = up_weight.shape[1]
    return pl.pallas_call(
        conv_up_kernel,
        grid_spec=pltpu.PrefetchScalarGridSpec(
            num_scalar_prefetch=1,
            grid=(members,),
            in_specs=[
                pl.BlockSpec((1, rows, width), lambda i, o: (i, 0, 0)),
                pl.BlockSpec((1, PAD, width), lambda i, o: (i, 0, 0)),
                pl.BlockSpec((1, PAD, width), lambda i, o: (i, 0, 0)),
                pl.BlockSpec((1, ROWS, rows), lambda i, o: (o[i], 0, 0)),
                pl.BlockSpec((width, units), lambda i, o: (i, 0)),
                pl.BlockSpec((rows, units), lambda i, o: (0, 0)),
            ],
            out_specs=[
                pl.BlockSpec((1, rows, width), lambda i, o: (i, 0, 0)),
                pl.BlockSpec((rows, units), lambda i, o: (0, 0)),
                pl.BlockSpec((rows, units), lambda i, o: (0, 0)),
            ],
            scratch_shapes=[
                pltpu.VMEM((rows + 64, width), BF16),
                pltpu.VMEM((rows, units), F32),
            ],
        ),
        out_shape=(
            jax.ShapeDtypeStruct((members, rows, width), BF16),
            jax.ShapeDtypeStruct((rows, units), BF16),
            jax.ShapeDtypeStruct((rows, units), BF16),
        ),
        compiler_params=params(40),
        name="conv_up",
    )(order, hidden_full, low, high, flat_full, up_weight, middle_grad)


def grad_middle_kernel(cot_ref, down_ref, out_ref):
    width = cot_ref.shape[2]
    total = jnp.zeros(out_ref.shape, F32)
    for piece in range(cot_ref.shape[0]):
        total = total + lax.dot_general(
            cot_ref[piece],
            down_ref[:, piece * width : (piece + 1) * width],
            NT,
            preferred_element_type=F32,
        )
    out_ref[...] = total


def grad_middle(cot_full, down_weight):
    pieces, rows, width = cot_full.shape
    units = down_weight.shape[0]
    block = 256
    return pl.pallas_call(
        grad_middle_kernel,
        grid=(units // block,),
        in_specs=[
            pl.BlockSpec((pieces, rows, width), lambda i: (0, 0, 0)),
            pl.BlockSpec((block, pieces * width), lambda i: (i, 0)),
        ],
        out_specs=pl.BlockSpec((rows, block), lambda i: (0, i)),
        out_shape=jax.ShapeDtypeStruct((rows, units), F32),
        compiler_params=params(40),
        name="grad_middle",
    )(cot_full, down_weight)


def spread_kernel(dims, order, value_ref, weight_ref, *out_refs):
    result = lax.dot_general(
        value_ref[...], weight_ref[...], dims, preferred_element_type=F32
    ).astype(BF16)
    for index, ref in enumerate(out_refs):

        @pl.when(lax.rem(pl.program_id(0), 4) == index)
        def _(ref=ref):
            ref[0] = result


def spread(order, value, weight, transposed, name):
    rows, units = value.shape
    if transposed:
        width = weight.shape[0] // 8
        spec = pl.BlockSpec((width, units), lambda k, o: (o[k], 0))
        dims = NT
    else:
        width = weight.shape[1] // 8
        spec = pl.BlockSpec((units, width), lambda k, o: (0, o[k]))
        dims = (((1,), (0,)), ((), ()))
    return pl.pallas_call(
        functools.partial(spread_kernel, dims),
        grid_spec=pltpu.PrefetchScalarGridSpec(
            num_scalar_prefetch=1,
            grid=(8,),
            in_specs=[pl.BlockSpec((rows, units), lambda k, o: (0, 0)), spec],
            out_specs=[pl.BlockSpec((1, rows, width), lambda k, o: (k // 4, 0, 0))] * 4,
        ),
        out_shape=[jax.ShapeDtypeStruct((2, rows, width), BF16)] * 4,
        compiler_params=params(40),
        name=name,
    )(order, value, weight)


def weight_grads_kernel(act_ref, cot_ref, pre_grad_ref, middle_ref, out_ref):
    up = lax.dot_general(act_ref[0], pre_grad_ref[...], TN, preferred_element_type=F32)
    down = lax.dot_general(cot_ref[0], middle_ref[...], TN, preferred_element_type=F32)
    chunk = out_ref.shape[1] // 2
    for index in range(out_ref.shape[0]):
        rows = slice(index * chunk, (index + 1) * chunk)
        out_ref[index, 0:chunk] = up[rows].astype(BF16)
        out_ref[index, chunk:] = down[rows].astype(BF16)


def weight_grads(act_full, cot_full, pre_grad, middle):
    pieces, rows, width = act_full.shape
    units = middle.shape[1]
    chunks = lax.axis_size("seq")
    per = chunks // pieces
    chunk = width // per
    return pl.pallas_call(
        weight_grads_kernel,
        grid=(pieces,),
        in_specs=[
            pl.BlockSpec((1, rows, width), lambda i: (i, 0, 0)),
            pl.BlockSpec((1, rows, width), lambda i: (i, 0, 0)),
            pl.BlockSpec((rows, units), lambda i: (0, 0)),
            pl.BlockSpec((rows, units), lambda i: (0, 0)),
        ],
        out_specs=pl.BlockSpec((per, 2 * chunk, units), lambda i: (i, 0, 0)),
        out_shape=jax.ShapeDtypeStruct((chunks, 2 * chunk, units), BF16),
        compiler_params=params(40),
        name="weight_grads",
    )(act_full, cot_full, pre_grad, middle)


def kernel_grad_kernel(*refs):
    terms = refs[:5]
    cot_ref, hidden_ref, low_ref, high_ref, tap_ref = refs[5:10]
    grad_ref, logit_ref, padded, found_ref = refs[10:]
    rows, width = hidden_ref.shape
    heads = 2
    head_width = width // heads
    padded[0:PAD] = low_ref[...].astype(F32)
    padded[PAD : PAD + rows] = hidden_ref[...].astype(F32)
    padded[PAD + rows :] = high_ref[...].astype(F32)
    step = 32
    lane = lax.broadcasted_iota(jnp.int32, (step, ROWS), 1)

    def run(index, carry):
        base = pl.multiple_of(index * step, step)
        at = pl.ds(base, step)
        grad = terms[0][at, :].astype(F32)
        for ref in terms[1:]:
            grad = grad + ref[at, :].astype(F32)
        grad = grad + cot_ref[at, :].astype(F32)
        grad_ref[at, :] = grad
        taps = tap_ref[at, :]
        found = jnp.zeros((step, ROWS), F32)
        for head in range(heads):
            lanes = slice(head * head_width, (head + 1) * head_width)
            window = padded[pl.ds(base, step + 2 * PAD), lanes]
            part = grad[:, lanes]
            for tap in range(KW):
                column = head * KW + tap
                value = jnp.sum(part * window[tap + 1 : tap + 1 + step], axis=1, keepdims=True)
                found = jnp.where(lane == column, value, found)
        product = taps * found
        in_first = lane < KW
        one = jnp.sum(jnp.where(in_first, product, 0.0), axis=1, keepdims=True)
        two = jnp.sum(jnp.where(in_first, 0.0, product), axis=1, keepdims=True)
        found_ref[at, :] = taps * (found - jnp.where(in_first, one, two))
        return carry

    lax.fori_loop(0, rows // step, run, 0)
    logit_ref[...] = found_ref[...].T.astype(BF16)


def kernel_grads(pairs, last, cotangent, hidden, low, high, taps):
    rows, width = hidden.shape
    flat = pl.BlockSpec((rows, width), lambda i: (0, 0))
    edge = pl.BlockSpec((PAD, width), lambda i: (0, 0))
    return pl.pallas_call(
        kernel_grad_kernel,
        grid=(1,),
        in_specs=[pl.BlockSpec((None, rows, width), lambda i: (0, 0, 0))] * 4
        + [flat, flat, flat, edge, edge, pl.BlockSpec((rows, ROWS), lambda i: (0, 0))],
        out_specs=[flat, pl.BlockSpec((ROWS, rows), lambda i: (0, 0))],
        out_shape=(
            jax.ShapeDtypeStruct((rows, width), F32),
            jax.ShapeDtypeStruct((ROWS, rows), BF16),
        ),
        scratch_shapes=[
            pltpu.VMEM((rows + 2 * PAD, width), F32),
            pltpu.VMEM((rows, ROWS), F32),
        ],
        compiler_params=params(32),
        name="kernel_grads",
    )(*pairs, last, cotangent, hidden, low, high, taps)


def hidden_grad_kernel(
    grad_ref,
    glow_ref,
    ghigh_ref,
    tap_ref,
    tlow_ref,
    thigh_ref,
    logit_ref,
    gen_ref,
    mask_ref,
    code_ref,
    embed_ref,
    table_ref,
    padded,
    tapped,
    back,
):
    rows, width = grad_ref.shape
    heads = 2
    head_width = width // heads
    padded[0:PAD] = glow_ref[...].astype(F32)
    padded[PAD : PAD + rows] = grad_ref[...]
    padded[PAD + rows :] = ghigh_ref[...].astype(F32)
    tapped[0:PAD] = tlow_ref[...]
    tapped[PAD : PAD + rows] = tap_ref[...]
    tapped[PAD + rows :] = thigh_ref[...]
    back[...] = lax.dot_general(logit_ref[...], gen_ref[...], TN, preferred_element_type=F32)
    step = 32

    def run(index, carry):
        base = pl.multiple_of(index * step, step)
        at = pl.ds(base, step)
        picked = mask_ref[at, :] == 1
        taps = tapped[pl.ds(base, step + 2 * PAD), :]
        for head in range(heads):
            lanes = slice(head * head_width, (head + 1) * head_width)
            window = padded[pl.ds(base, step + 2 * PAD), lanes]
            total = window[PAD : PAD + step] + back[at, lanes]
            for tap in range(KW):
                column = head * KW + tap
                lower = 2 * PAD - 1 - tap
                total = (
                    total
                    + taps[lower : lower + step, column : column + 1]
                    * window[lower : lower + step]
                )
            embed_ref[at, lanes] = jnp.where(picked, 0.0, total)
            back[at, lanes] = jnp.where(picked, total, 0.0)
        return carry

    lax.fori_loop(0, rows // step, run, 0)
    codes = lax.broadcasted_iota(jnp.int32, (table_ref.shape[0], rows), 0)
    chosen = jnp.where(codes == code_ref[...], 1.0, 0.0).astype(BF16)
    value = back[...]
    upper = value.astype(BF16)
    lower = (value - upper.astype(F32)).astype(BF16)
    table_ref[...] = jnp.dot(chosen, upper, preferred_element_type=F32) + jnp.dot(
        chosen, lower, preferred_element_type=F32
    )


def hidden_grads(grad, glow, ghigh, taps, tlow, thigh, logit_full, gen_full, mask, code, codes):
    rows, width = grad.shape
    return pl.pallas_call(
        hidden_grad_kernel,
        out_shape=(
            jax.ShapeDtypeStruct((rows, width), F32),
            jax.ShapeDtypeStruct((codes, width), F32),
        ),
        scratch_shapes=[
            pltpu.VMEM((rows + 2 * PAD, width), F32),
            pltpu.VMEM((rows + 2 * PAD, ROWS), F32),
            pltpu.VMEM((rows, width), F32),
        ],
        compiler_params=params(32),
        name="hidden_grads",
    )(grad, glow, ghigh, taps, tlow, thigh, logit_full, gen_full, mask, code)


def gen_grads_kernel(logit_ref, hidden_ref, out_ref):
    width = hidden_ref.shape[2]
    for piece in range(hidden_ref.shape[0]):
        out_ref[:, piece * width : (piece + 1) * width] = jnp.dot(
            logit_ref[...], hidden_ref[piece], preferred_element_type=F32
        )


def gen_grads(logit_grad, hidden_full):
    members, rows, width = hidden_full.shape
    heads = logit_grad.shape[0]
    return pl.pallas_call(
        gen_grads_kernel,
        out_shape=jax.ShapeDtypeStruct((heads, members * width), F32),
        compiler_params=params(32),
        name="gen_grads",
    )(logit_grad, hidden_full)


def after(value, *others):
    return lax.optimization_barrier((value, *others))[0]


def add_pairs(pairs, index):
    total = pairs[0][index].astype(F32)
    for pair in pairs[1:]:
        total = total + pair[index].astype(F32)
    return total


def swap_pairs(pairs):
    return [pairs[0]] + [flip(pairs[z], "tp", z) for z in (1, 2, 3)]


def body(
    embeddings,
    span_mask,
    sentinel_id,
    sentinel_table,
    gen_weight,
    up_weight,
    down_weight,
    cotangent,
):
    rows, width = embeddings.shape
    codes = sentinel_table.shape[0]
    members = lax.axis_size("tp")
    me = lax.axis_index("tp")
    order = jnp.arange(members, dtype=jnp.int32) ^ me.astype(jnp.int32)

    sentinel_codes = jnp.arange(codes, dtype=jnp.int32)
    onehot = (sentinel_id[:, None] == sentinel_codes[None, :]).astype(BF16)
    picked = jnp.dot(onehot, sentinel_table, preferred_element_type=F32).astype(BF16)
    hidden = jnp.where(span_mask[:, None] == 1, picked, embeddings)
    pieces = gather_pieces(hidden)
    cot_full = lax.all_gather(cotangent, "tp", axis=0, tiled=False)

    hidden_full, edges, flat, taps = hidden_logits(order, pieces, gen_weight.T)
    high_full, low_full = edges[0], edges[1]
    count = lax.axis_size("seq")
    low_full = lax.ppermute(low_full, "seq", [(i, i + 1) for i in range(count - 1)])
    high_full = lax.ppermute(high_full, "seq", [(i + 1, i) for i in range(count - 1)])
    flat_full = gather_small(flat)
    middle_grad = grad_middle(cot_full, down_weight)
    act_full, middle, pre_grad = conv_up(
        order, hidden_full, low_full, high_full, flat_full, up_weight, middle_grad
    )

    summed = weight_grads(act_full, cot_full, pre_grad, middle)
    back_pairs = swap_pairs(spread(order, pre_grad, up_weight, True, "act_back"))
    summed = lax.psum_scatter(summed, "seq", scatter_dimension=0, tiled=False)
    out_pairs = spread(order, middle, down_weight, False, "ffn_out")

    columns = gen_weight.shape[1]
    gen_rows = jnp.pad(gen_weight.T, ((0, ROWS - columns), (0, 0)))
    gen_own = jnp.stack(
        [
            lax.dynamic_slice(gen_rows, (jnp.int32(0), order[k] * width), (ROWS, width))
            for k in range(members)
        ]
    )
    gen_full = exchange(after(gen_own, pre_grad)).reshape(members * ROWS, width)
    tap_low, tap_high = halo(taps)

    back_last = flip(add_pairs(back_pairs, 1).astype(BF16), "tp", 4)
    low = lax.dynamic_index_in_dim(low_full, me, 0, keepdims=False)
    high = lax.dynamic_index_in_dim(high_full, me, 0, keepdims=False)
    grad, logit_grad = kernel_grads(
        back_pairs, back_last, after(cotangent, *out_pairs, gen_full), hidden, low, high, taps
    )
    grad_low, grad_high = halo(grad.astype(BF16))
    logit_full = gather_small(logit_grad).reshape(members * ROWS, rows)
    embed_grad, table_part = hidden_grads(
        grad,
        grad_low,
        grad_high,
        taps,
        tap_low,
        tap_high,
        logit_full,
        gen_full,
        span_mask[:, None],
        sentinel_id[None, :],
        codes,
    )
    gen_sum = sum_over_seq(gen_grads(logit_grad, hidden_full))
    gen_grad = gen_sum[:columns].T
    table_grad = sum_over_seq(table_part)

    out_pairs = swap_pairs([after(pair, grad) for pair in out_pairs])
    total = add_pairs(out_pairs, 0) + flip(
        add_pairs(out_pairs, 1).astype(BF16), "tp", 4
    ).astype(F32)
    act = lax.dynamic_index_in_dim(act_full, me, 0, keepdims=False)
    layer_output = (act.astype(F32) + total).astype(BF16)

    chunk = summed.shape[0] // 2
    up_grad = summed[:chunk].astype(F32)
    down_grad = summed[chunk:].astype(F32).T
    return (layer_output, embed_grad, table_grad, gen_grad, up_grad, down_grad)


def solution(mesh):
    placed = (
        P("seq", "tp"),
        P("seq"),
        P("seq"),
        P(None, "tp"),
        P(None, "tp"),
        P(None, "tp"),
        P("tp", None),
        P("seq", "tp"),
    )
    return jax.shard_map(
        body,
        mesh=mesh,
        in_specs=placed,
        out_specs=(
            P("seq", "tp"),
            P("seq", "tp"),
            P(None, "tp"),
            P(None, "tp"),
            P("seq", "tp"),
            P("tp", "seq"),
        ),
        check_vma=False,
    )
```

```python
import functools

import jax
import jax.numpy as jnp
from jax import lax
from jax.experimental import pallas as pl
from jax.experimental.pallas import tpu as pltpu
from jax.sharding import PartitionSpec as P

KW = 15
REACH = 7
PAD = 8
ROWS = 32
F32 = jnp.float32
BF16 = jnp.bfloat16
NT = (((1,), (1,)), ((), ()))
TN = (((0,), (0,)), ((), ()))


def params(megabytes=60):
    return pltpu.CompilerParams(vmem_limit_bytes=megabytes << 20)


def after(value, *others):
    return lax.optimization_barrier((value, *others))[0]


def ordered(kernel, inputs, tokens):
    def run(*refs):
        kernel(*refs[:inputs], *refs[inputs + len(tokens) :])

    return run, [pl.BlockSpec(memory_space=pl.ANY) for _ in tokens]


def flip(value, axis, bit):
    count = lax.axis_size(axis)
    return lax.ppermute(value, axis, [(i, i ^ bit) for i in range(count)])


def halo(value):
    count = lax.axis_size("seq")
    forward = [(i, i + 1) for i in range(count - 1)]
    backward = [(i + 1, i) for i in range(count - 1)]
    low = lax.ppermute(value[-PAD:], "seq", forward)
    high = lax.ppermute(value[:PAD], "seq", backward)
    return low, high


def exchange(blocks, bits=(4, 2, 1)):
    shape = blocks.shape
    cube = blocks.reshape((2, 2, 2) + shape[1:])
    for bit in bits:
        place = {4: 0, 2: 1, 1: 2}[bit]
        keep = lax.index_in_dim(cube, 0, place, keepdims=True)
        send = lax.index_in_dim(cube, 1, place, keepdims=True)
        cube = jnp.concatenate([keep, flip(send, "tp", bit)], axis=place)
    return cube.reshape(shape)


def gather_small(value, beside=()):
    blocks = value[None]
    for bit in (1, 2, 4):
        other = flip(blocks, "tp", bit)
        if bit == 4 and beside:
            other = after(other, *beside)
        blocks = jnp.concatenate([blocks, other], axis=0)
    return blocks


def sum_over_seq(value, bits=(1, 8, 2, 4)):
    for bit in bits:
        sent = value.astype(BF16)
        value = sent.astype(F32) + flip(sent, "seq", bit).astype(F32)
    return value


def gather_pieces(value):
    half = value.shape[0] // 2
    four = flip(value, "tp", 4)
    one = flip(value, "tp", 1)
    three = flip(value, "tp", 3)
    five = flip(four, "tp", 1)
    seven = flip(four, "tp", 3)
    two_a = flip(one[:half], "tp", 3)
    two_b = flip(three[half:], "tp", 1)
    six_a = flip(five[:half], "tp", 3)
    six_b = flip(seven[half:], "tp", 1)
    return value, one, three, four, five, seven, two_a, two_b, six_a, six_b


def hidden_logits_kernel(order, *refs):
    pieces = refs[:10]
    gen_ref, full_ref, edge_ref, flat_ref, tap_ref, sems = refs[10:]
    members, rows, width = full_ref.shape
    half = rows // 2
    targets = [full_ref.at[order[at]] for at in (0, 1, 3, 4, 5, 7)]
    for at in (2, 6):
        targets.append(full_ref.at[order[at], 0:half])
        targets.append(full_ref.at[order[at], half:rows])
    copies = [
        pltpu.make_async_copy(ref, target, sems.at[index])
        for index, (ref, target) in enumerate(zip(pieces, targets))
    ]
    for copy in copies:
        copy.start()
    for copy in copies:
        copy.wait()
    logits = jnp.zeros((gen_ref.shape[0], rows), F32)
    for piece in range(members):
        edge_ref[0, piece] = full_ref[piece, 0:PAD]
        edge_ref[1, piece] = full_ref[piece, rows - PAD :]
        logits = logits + lax.dot_general(
            gen_ref[:, piece * width : (piece + 1) * width],
            full_ref[piece],
            NT,
            preferred_element_type=F32,
        )
    exps = jnp.exp(logits)
    first = exps[0:KW]
    second = exps[KW : 2 * KW]
    first = first / jnp.sum(first, axis=0, keepdims=True)
    second = second / jnp.sum(second, axis=0, keepdims=True)
    blank = jnp.zeros((ROWS - 2 * KW, rows), F32)
    flat = jnp.concatenate([first, second, blank], axis=0)
    flat_ref[...] = flat
    tap_ref[...] = flat.T


def hidden_logits(order, pieces, gen_rows):
    rows, width = pieces[0].shape
    columns, depth = gen_rows.shape
    members = depth // width
    whole = [pl.BlockSpec(memory_space=pltpu.HBM) for _ in pieces]
    return pl.pallas_call(
        hidden_logits_kernel,
        grid_spec=pltpu.PrefetchScalarGridSpec(
            num_scalar_prefetch=1,
            grid=(1,),
            in_specs=whole + [pl.BlockSpec((columns, depth), lambda i, o: (0, 0))],
            out_specs=[
                pl.BlockSpec((members, rows, width), lambda i, o: (0, 0, 0)),
                pl.BlockSpec((2, members, PAD, width), lambda i, o: (0, 0, 0, 0)),
                pl.BlockSpec((ROWS, rows), lambda i, o: (0, 0)),
                pl.BlockSpec((rows, ROWS), lambda i, o: (0, 0)),
            ],
            scratch_shapes=[pltpu.SemaphoreType.DMA((len(pieces),))],
        ),
        out_shape=(
            jax.ShapeDtypeStruct((members, rows, width), BF16),
            jax.ShapeDtypeStruct((2, members, PAD, width), BF16),
            jax.ShapeDtypeStruct((ROWS, rows), F32),
            jax.ShapeDtypeStruct((rows, ROWS), F32),
        ),
        compiler_params=params(),
        name="hidden_logits",
    )(order, *pieces, gen_rows)


def conv_up_kernel(
    order,
    hidden_ref,
    low_ref,
    high_ref,
    flat_one_ref,
    flat_two_ref,
    up_ref,
    grad_ref,
    act_ref,
    middle_ref,
    pre_grad_ref,
    padded,
    pre,
):
    count, rows, width = hidden_ref.shape
    step = 64
    reach = 2 * step
    heads = 2
    head_width = width // heads
    lane = lax.broadcasted_iota(jnp.int32, (step, reach), 1)
    term = None
    for piece, flat_ref in enumerate((flat_one_ref, flat_two_ref)):
        padded[piece, 0:PAD] = low_ref[piece]
        padded[piece, PAD : PAD + rows] = hidden_ref[piece]
        padded[piece, PAD + rows : 2 * PAD + rows] = high_ref[piece]
        padded[piece, 2 * PAD + rows :] = jnp.zeros((step - 2 * PAD, width), BF16)
        flat = flat_ref[0]
        taps = jnp.concatenate([flat, jnp.zeros((reach - ROWS, rows), F32)], axis=0).T
        for base in range(0, rows, step):
            for head in range(heads):
                lanes = slice(head * head_width, (head + 1) * head_width)
                mine = (lane >= head * KW) & (lane < (head + 1) * KW)
                own = jnp.where(mine, taps[base : base + step], 0.0)
                own = pltpu.roll(own, (1 - head * KW) % reach, 1)
                band = pltpu.roll(own, 0, 1, stride=1, stride_axis=0)
                upper = band.astype(BF16)
                lower = (band - upper.astype(F32)).astype(BF16)
                window = padded[piece, base : base + reach, lanes]
                both = jnp.dot(
                    jnp.concatenate([upper, lower], axis=0), window, preferred_element_type=F32
                )
                value = hidden_ref[piece, base : base + step, lanes].astype(F32)
                value = value + (both[:step] + both[step:])
                act_ref[piece, base : base + step, lanes] = value.astype(BF16)
        part = jnp.dot(
            act_ref[piece],
            up_ref[piece * width : (piece + 1) * width, :],
            preferred_element_type=F32,
        )
        term = part if term is None else term + part

    @pl.when(pl.program_id(0) == 0)
    def _():
        pre[...] = term

    @pl.when(pl.program_id(0) > 0)
    def _():
        pre[...] += term

    @pl.when(pl.program_id(0) == pl.num_programs(0) - 1)
    def _():
        scale = 0.7978845608028654
        chunk = 64

        def run(index, carry):
            at = pl.ds(pl.multiple_of(index * chunk, chunk), chunk)
            value = pre[at, :]
            square = value * value
            bent = jnp.tanh(scale * (value + 0.044715 * (square * value)))
            middle_ref[at, :] = (0.5 * value * (1.0 + bent)).astype(BF16)
            slope = 0.5 * (1.0 + bent) + 0.5 * value * (1.0 - bent * bent) * (
                scale * (1.0 + 3.0 * 0.044715 * square)
            )
            pre_grad_ref[at, :] = (grad_ref[at, :] * slope).astype(BF16)
            return carry

        lax.fori_loop(0, rows // chunk, run, 0)


def conv_up(order, hidden_full, low, high, flat_full, up_weight, middle_grad):
    members, rows, width = hidden_full.shape
    units = up_weight.shape[1]
    return pl.pallas_call(
        conv_up_kernel,
        grid_spec=pltpu.PrefetchScalarGridSpec(
            num_scalar_prefetch=1,
            grid=(members // 2,),
            in_specs=[
                pl.BlockSpec((2, rows, width), lambda i, o: (i, 0, 0)),
                pl.BlockSpec((2, PAD, width), lambda i, o: (i, 0, 0)),
                pl.BlockSpec((2, PAD, width), lambda i, o: (i, 0, 0)),
                pl.BlockSpec((1, ROWS, rows), lambda i, o: (o[2 * i], 0, 0)),
                pl.BlockSpec((1, ROWS, rows), lambda i, o: (o[2 * i + 1], 0, 0)),
                pl.BlockSpec((2 * width, units), lambda i, o: (i, 0)),
                pl.BlockSpec((rows, units), lambda i, o: (0, 0)),
            ],
            out_specs=[
                pl.BlockSpec((2, rows, width), lambda i, o: (i, 0, 0)),
                pl.BlockSpec((rows, units), lambda i, o: (0, 0)),
                pl.BlockSpec((rows, units), lambda i, o: (0, 0)),
            ],
            scratch_shapes=[
                pltpu.VMEM((2, rows + 64, width), BF16),
                pltpu.VMEM((rows, units), F32),
            ],
        ),
        out_shape=(
            jax.ShapeDtypeStruct((members, rows, width), BF16),
            jax.ShapeDtypeStruct((rows, units), BF16),
            jax.ShapeDtypeStruct((rows, units), BF16),
        ),
        compiler_params=params(),
        name="conv_up",
    )(order, hidden_full, low, high, flat_full, flat_full, up_weight, middle_grad)


def grad_middle_kernel(cot_ref, down_ref, out_ref):
    width = cot_ref.shape[2]
    total = jnp.zeros(out_ref.shape, F32)
    for piece in range(cot_ref.shape[0]):
        total = total + lax.dot_general(
            cot_ref[piece],
            down_ref[:, piece * width : (piece + 1) * width],
            NT,
            preferred_element_type=F32,
        )
    out_ref[...] = total


def grad_middle(cot_full, down_weight):
    pieces, rows, width = cot_full.shape
    units = down_weight.shape[0]
    block = 256
    return pl.pallas_call(
        grad_middle_kernel,
        grid=(units // block,),
        in_specs=[
            pl.BlockSpec((pieces, rows, width), lambda i: (0, 0, 0)),
            pl.BlockSpec((block, pieces * width), lambda i: (i, 0)),
        ],
        out_specs=pl.BlockSpec((rows, block), lambda i: (0, i)),
        out_shape=jax.ShapeDtypeStruct((rows, units), F32),
        compiler_params=params(),
        name="grad_middle",
    )(cot_full, down_weight)


def spread_kernel(dims, order, value_ref, weight_ref, *out_refs):
    result = lax.dot_general(
        value_ref[...], weight_ref[...], dims, preferred_element_type=F32
    ).astype(BF16)
    for index, ref in enumerate(out_refs):

        @pl.when(lax.rem(pl.program_id(0), 4) == index)
        def _(ref=ref):
            ref[0] = result


def spread(order, value, weight, transposed, name):
    rows, units = value.shape
    if transposed:
        width = weight.shape[0] // 8
        spec = pl.BlockSpec((width, units), lambda k, o: (o[k], 0))
        dims = NT
    else:
        width = weight.shape[1] // 8
        spec = pl.BlockSpec((units, width), lambda k, o: (0, o[k]))
        dims = (((1,), (0,)), ((), ()))
    return pl.pallas_call(
        functools.partial(spread_kernel, dims),
        grid_spec=pltpu.PrefetchScalarGridSpec(
            num_scalar_prefetch=1,
            grid=(8,),
            in_specs=[pl.BlockSpec((rows, units), lambda k, o: (0, 0)), spec],
            out_specs=[pl.BlockSpec((1, rows, width), lambda k, o: (k // 4, 0, 0))] * 4,
        ),
        out_shape=[jax.ShapeDtypeStruct((2, rows, width), BF16)] * 4,
        compiler_params=params(),
        name=name,
    )(order, value, weight)


def halves_kernel(order, value_ref, weight_ref, near_ref, far_ref):
    result = jnp.dot(value_ref[...], weight_ref[...], preferred_element_type=F32).astype(BF16)

    @pl.when(pl.program_id(0) < 4)
    def _():
        far_ref[0] = result

    @pl.when(pl.program_id(0) >= 4)
    def _():
        near_ref[0] = result


def halves(order, value, weight, tokens):
    rows, units = value.shape
    width = weight.shape[1] // 8
    kernel, token_specs = ordered(halves_kernel, 3, tokens)
    return pl.pallas_call(
        kernel,
        grid_spec=pltpu.PrefetchScalarGridSpec(
            num_scalar_prefetch=1,
            grid=(8,),
            in_specs=[
                pl.BlockSpec((rows, units), lambda k, o: (0, 0)),
                pl.BlockSpec((units, width), lambda k, o: (0, o[(k + 4) % 8])),
            ]
            + token_specs,
            out_specs=[
                pl.BlockSpec((1, rows, width), lambda k, o: (jnp.maximum(k - 4, 0), 0, 0)),
                pl.BlockSpec((1, rows, width), lambda k, o: (jnp.minimum(k, 3), 0, 0)),
            ],
        ),
        out_shape=[jax.ShapeDtypeStruct((4, rows, width), BF16)] * 2,
        compiler_params=params(),
        name="ffn_out",
    )(order, value, weight, *tokens)


def weight_grads_kernel(act_ref, cot_ref, pre_grad_ref, middle_ref, out_ref):
    up = lax.dot_general(act_ref[0], pre_grad_ref[...], TN, preferred_element_type=F32)
    down = lax.dot_general(cot_ref[0], middle_ref[...], TN, preferred_element_type=F32)
    chunk = out_ref.shape[1] // 2
    for index in range(out_ref.shape[0]):
        rows = slice(index * chunk, (index + 1) * chunk)
        out_ref[index, 0:chunk] = up[rows].astype(BF16)
        out_ref[index, chunk:] = down[rows].astype(BF16)


def weight_grads(act_full, cot_full, pre_grad, middle):
    pieces, rows, width = act_full.shape
    units = middle.shape[1]
    chunks = lax.axis_size("seq")
    per = chunks // pieces
    chunk = width // per
    return pl.pallas_call(
        weight_grads_kernel,
        grid=(pieces,),
        in_specs=[
            pl.BlockSpec((1, rows, width), lambda i: (i, 0, 0)),
            pl.BlockSpec((1, rows, width), lambda i: (i, 0, 0)),
            pl.BlockSpec((rows, units), lambda i: (0, 0)),
            pl.BlockSpec((rows, units), lambda i: (0, 0)),
        ],
        out_specs=pl.BlockSpec((per, 2 * chunk, units), lambda i: (i, 0, 0)),
        out_shape=jax.ShapeDtypeStruct((chunks, 2 * chunk, units), BF16),
        compiler_params=params(),
        name="weight_grads",
    )(act_full, cot_full, pre_grad, middle)


def kernel_grad_kernel(*refs):
    terms = refs[:5]
    cot_ref, hidden_ref, low_ref, high_ref, tap_ref = refs[5:10]
    grad_ref, logit_ref, padded, found_ref = refs[10:]
    rows, width = hidden_ref.shape
    heads = 2
    head_width = width // heads
    padded[0:PAD] = low_ref[...].astype(F32)
    padded[PAD : PAD + rows] = hidden_ref[...].astype(F32)
    padded[PAD + rows :] = high_ref[...].astype(F32)
    step = 32
    lane = lax.broadcasted_iota(jnp.int32, (step, ROWS), 1)

    def run(index, carry):
        base = pl.multiple_of(index * step, step)
        at = pl.ds(base, step)
        grad = terms[0][at, :].astype(F32)
        for ref in terms[1:]:
            grad = grad + ref[at, :].astype(F32)
        grad = grad + cot_ref[at, :].astype(F32)
        grad_ref[at, :] = grad
        taps = tap_ref[at, :]
        found = jnp.zeros((step, ROWS), F32)
        for head in range(heads):
            lanes = slice(head * head_width, (head + 1) * head_width)
            window = padded[pl.ds(base, step + 2 * PAD), lanes]
            part = grad[:, lanes]
            for tap in range(KW):
                column = head * KW + tap
                value = jnp.sum(part * window[tap + 1 : tap + 1 + step], axis=1, keepdims=True)
                found = jnp.where(lane == column, value, found)
        product = taps * found
        in_first = lane < KW
        one = jnp.sum(jnp.where(in_first, product, 0.0), axis=1, keepdims=True)
        two = jnp.sum(jnp.where(in_first, 0.0, product), axis=1, keepdims=True)
        found_ref[at, :] = taps * (found - jnp.where(in_first, one, two))
        return carry

    lax.fori_loop(0, rows // step, run, 0)
    logit_ref[...] = found_ref[...].T.astype(BF16)


def kernel_grads(pairs, last, cotangent, hidden, low, high, taps, tokens):
    rows, width = hidden.shape
    flat = pl.BlockSpec((rows, width), lambda i: (0, 0))
    edge = pl.BlockSpec((PAD, width), lambda i: (0, 0))
    kernel, token_specs = ordered(kernel_grad_kernel, 10, tokens)
    return pl.pallas_call(
        kernel,
        grid=(1,),
        in_specs=[pl.BlockSpec((None, rows, width), lambda i: (0, 0, 0))] * 4
        + [flat, flat, flat, edge, edge, pl.BlockSpec((rows, ROWS), lambda i: (0, 0))]
        + token_specs,
        out_specs=[flat, pl.BlockSpec((ROWS, rows), lambda i: (0, 0))],
        out_shape=(
            jax.ShapeDtypeStruct((rows, width), F32),
            jax.ShapeDtypeStruct((ROWS, rows), BF16),
        ),
        scratch_shapes=[
            pltpu.VMEM((rows + 2 * PAD, width), F32),
            pltpu.VMEM((rows, ROWS), F32),
        ],
        compiler_params=params(24),
        name="kernel_grads",
    )(*pairs, last, cotangent, hidden, low, high, taps, *tokens)


def hidden_grad_kernel(
    grad_ref,
    glow_ref,
    ghigh_ref,
    tap_ref,
    tlow_ref,
    thigh_ref,
    logit_ref,
    gen_ref,
    mask_ref,
    code_ref,
    embed_ref,
    table_ref,
    padded,
    tapped,
    back,
):
    rows, width = grad_ref.shape
    heads = 2
    head_width = width // heads
    padded[0:PAD] = glow_ref[...].astype(F32)
    padded[PAD : PAD + rows] = grad_ref[...]
    padded[PAD + rows :] = ghigh_ref[...].astype(F32)
    tapped[0:PAD] = tlow_ref[...]
    tapped[PAD : PAD + rows] = tap_ref[...]
    tapped[PAD + rows :] = thigh_ref[...]
    back[...] = lax.dot_general(logit_ref[...], gen_ref[...], TN, preferred_element_type=F32)
    step = 32

    def run(index, carry):
        base = pl.multiple_of(index * step, step)
        at = pl.ds(base, step)
        picked = mask_ref[at, :] == 1
        taps = tapped[pl.ds(base, step + 2 * PAD), :]
        for head in range(heads):
            lanes = slice(head * head_width, (head + 1) * head_width)
            window = padded[pl.ds(base, step + 2 * PAD), lanes]
            total = window[PAD : PAD + step] + back[at, lanes]
            for tap in range(KW):
                column = head * KW + tap
                lower = 2 * PAD - 1 - tap
                total = (
                    total
                    + taps[lower : lower + step, column : column + 1]
                    * window[lower : lower + step]
                )
            embed_ref[at, lanes] = jnp.where(picked, 0.0, total)
            back[at, lanes] = jnp.where(picked, total, 0.0)
        return carry

    lax.fori_loop(0, rows // step, run, 0)
    codes = lax.broadcasted_iota(jnp.int32, (table_ref.shape[0], rows), 0)
    chosen = jnp.where(codes == code_ref[...], 1.0, 0.0).astype(BF16)
    value = back[...]
    upper = value.astype(BF16)
    lower = (value - upper.astype(F32)).astype(BF16)
    table_ref[...] = jnp.dot(chosen, upper, preferred_element_type=F32) + jnp.dot(
        chosen, lower, preferred_element_type=F32
    )


def hidden_grads(operands, codes, tokens):
    rows, width = operands[0].shape
    kernel, token_specs = ordered(hidden_grad_kernel, len(operands), tokens)
    whole = [pl.BlockSpec(o.shape, lambda i: (0, 0)) for o in operands]
    return pl.pallas_call(
        kernel,
        grid=(1,),
        in_specs=whole + token_specs,
        out_specs=[
            pl.BlockSpec((rows, width), lambda i: (0, 0)),
            pl.BlockSpec((codes, width), lambda i: (0, 0)),
        ],
        out_shape=(
            jax.ShapeDtypeStruct((rows, width), F32),
            jax.ShapeDtypeStruct((codes, width), F32),
        ),
        scratch_shapes=[
            pltpu.VMEM((rows + 2 * PAD, width), F32),
            pltpu.VMEM((rows + 2 * PAD, ROWS), F32),
            pltpu.VMEM((rows, width), F32),
        ],
        compiler_params=params(24),
        name="hidden_grads",
    )(*operands, *tokens)


def gen_blocks_kernel(order, gen_ref, token_ref, out_ref):
    columns = gen_ref.shape[0]
    members, _, width = out_ref.shape
    out_ref[...] = jnp.zeros_like(out_ref)
    for k in range(members):
        at = pl.multiple_of(order[k] * width, width)
        out_ref[k, 0:columns] = gen_ref[:, pl.ds(at, width)]


def gen_blocks(order, gen_rows, width, token):
    columns, depth = gen_rows.shape
    members = depth // width
    return pl.pallas_call(
        gen_blocks_kernel,
        grid_spec=pltpu.PrefetchScalarGridSpec(
            num_scalar_prefetch=1,
            grid=(1,),
            in_specs=[
                pl.BlockSpec((columns, depth), lambda i, o: (0, 0)),
                pl.BlockSpec(memory_space=pl.ANY),
            ],
            out_specs=pl.BlockSpec((members, ROWS, width), lambda i, o: (0, 0, 0)),
        ),
        out_shape=jax.ShapeDtypeStruct((members, ROWS, width), BF16),
        compiler_params=params(24),
        name="gen_blocks",
    )(order, gen_rows, token)


def gen_grads_kernel(logit_ref, hidden_ref, out_ref):
    width = hidden_ref.shape[2]
    for piece in range(hidden_ref.shape[0]):
        out_ref[:, piece * width : (piece + 1) * width] = jnp.dot(
            logit_ref[...], hidden_ref[piece], preferred_element_type=F32
        )


def gen_grads(logit_grad, hidden_full):
    members, rows, width = hidden_full.shape
    heads = logit_grad.shape[0]
    return pl.pallas_call(
        gen_grads_kernel,
        out_shape=jax.ShapeDtypeStruct((heads, members * width), F32),
        compiler_params=params(24),
        name="gen_grads",
    )(logit_grad, hidden_full)


def add_up(values):
    total = values[0].astype(F32)
    for value in values[1:]:
        total = total + value.astype(F32)
    return total


def swap_pairs(pairs):
    return [pairs[0]] + [flip(pairs[z], "tp", z) for z in (1, 2, 3)]


def body(
    embeddings,
    span_mask,
    sentinel_id,
    sentinel_table,
    gen_weight,
    up_weight,
    down_weight,
    cotangent,
):
    rows, width = embeddings.shape
    codes = sentinel_table.shape[0]
    members = lax.axis_size("tp")
    me = lax.axis_index("tp")
    order = jnp.arange(members, dtype=jnp.int32) ^ me.astype(jnp.int32)

    sentinel_codes = jnp.arange(codes, dtype=jnp.int32)
    onehot = (sentinel_id[:, None] == sentinel_codes[None, :]).astype(BF16)
    picked = jnp.dot(onehot, sentinel_table, preferred_element_type=F32).astype(BF16)
    hidden = jnp.where(span_mask[:, None] == 1, picked, embeddings)
    pieces = gather_pieces(hidden)
    cot_full = lax.all_gather(cotangent, "tp", axis=0, tiled=False)

    hidden_full, edges, flat, taps = hidden_logits(order, pieces, gen_weight.T)
    high_full, low_full = edges[0], edges[1]
    count = lax.axis_size("seq")
    low_full = lax.ppermute(low_full, "seq", [(i, i + 1) for i in range(count - 1)])
    high_full = lax.ppermute(high_full, "seq", [(i + 1, i) for i in range(count - 1)])
    middle_grad = grad_middle(cot_full, down_weight)
    flat_full = gather_small(flat, (middle_grad,))
    act_full, middle, pre_grad = conv_up(
        order, hidden_full, low_full, high_full, flat_full, up_weight, middle_grad
    )

    summed = weight_grads(act_full, cot_full, pre_grad, middle)
    back_own = spread(order, pre_grad, up_weight, True, "act_back")
    back_pairs = swap_pairs(back_own)
    summed = lax.psum_scatter(summed, "seq", scatter_dimension=0, tiled=False)
    columns = gen_weight.shape[1]
    gen_full = gen_blocks(order, gen_weight.T, width, back_own[0])
    out_near, out_far = halves(order, middle, down_weight, (back_pairs[1],))
    out_far = flip(out_far, "tp", 4)

    gen_full = exchange(gen_full).reshape(members * ROWS, width)
    tap_low, tap_high = halo(taps)

    back_last = flip(add_up([pair[1] for pair in back_pairs]).astype(BF16), "tp", 4)
    low = lax.dynamic_index_in_dim(low_full, me, 0, keepdims=False)
    high = lax.dynamic_index_in_dim(high_full, me, 0, keepdims=False)
    grad, logit_grad = kernel_grads(
        back_pairs,
        back_last,
        cotangent,
        hidden,
        low,
        high,
        taps,
        (out_far, gen_full, tap_low, tap_high),
    )
    grad_low, grad_high = halo(grad.astype(BF16))
    logit_full = gather_small(logit_grad).reshape(members * ROWS, rows)
    gen_sum = sum_over_seq(gen_grads(logit_grad, hidden_full), (1, 8))
    out_sums = [add_up([out_near[z], out_far[z]]) for z in range(members // 2)]
    out_one, out_two, out_three = [flip(out_sums[z].astype(BF16), "tp", z) for z in (1, 2, 3)]
    embed_grad, table_part = hidden_grads(
        (
            grad,
            grad_low,
            grad_high,
            taps,
            tap_low,
            tap_high,
            logit_full,
            gen_full,
            span_mask[:, None],
            sentinel_id[None, :],
        ),
        codes,
        (gen_sum, out_one, out_three),
    )
    gen_sum = sum_over_seq(gen_sum, (2, 4))
    gen_grad = gen_sum[:columns].T
    table_grad = sum_over_seq(table_part)

    total = add_up([out_sums[0], out_one, out_two, out_three])
    act = lax.dynamic_index_in_dim(act_full, me, 0, keepdims=False)
    layer_output = (act.astype(F32) + total).astype(BF16)

    chunk = summed.shape[0] // 2
    up_grad = summed[:chunk].astype(F32)
    down_grad = summed[chunk:].astype(F32).T
    return (layer_output, embed_grad, table_grad, gen_grad, up_grad, down_grad)


def solution(mesh):
    placed = (
        P("seq", "tp"),
        P("seq"),
        P("seq"),
        P(None, "tp"),
        P(None, "tp"),
        P(None, "tp"),
        P("tp", None),
        P("seq", "tp"),
    )
    return jax.shard_map(
        body,
        mesh=mesh,
        in_specs=placed,
        out_specs=(
            P("seq", "tp"),
            P("seq", "tp"),
            P(None, "tp"),
            P(None, "tp"),
            P("seq", "tp"),
            P("tp", "seq"),
        ),
        check_vma=False,
    )
```

```python
import functools

import jax
import jax.numpy as jnp
from jax import lax
from jax.experimental import pallas as pl
from jax.experimental.pallas import tpu as pltpu
from jax.sharding import PartitionSpec as P

KW = 15
REACH = 7
PAD = 8
ROWS = 32
F32 = jnp.float32
BF16 = jnp.bfloat16
NT = (((1,), (1,)), ((), ()))
TN = (((0,), (0,)), ((), ()))


def params(megabytes=60):
    return pltpu.CompilerParams(vmem_limit_bytes=megabytes << 20)


def after(value, *others):
    return lax.optimization_barrier((value, *others))[0]


def ordered(kernel, inputs, tokens):
    def run(*refs):
        kernel(*refs[:inputs], *refs[inputs + len(tokens) :])

    return run, [pl.BlockSpec(memory_space=pl.ANY) for _ in tokens]


def flip(value, axis, bit):
    count = lax.axis_size(axis)
    return lax.ppermute(value, axis, [(i, i ^ bit) for i in range(count)])


def halo(value):
    count = lax.axis_size("seq")
    forward = [(i, i + 1) for i in range(count - 1)]
    backward = [(i + 1, i) for i in range(count - 1)]
    low = lax.ppermute(value[-PAD:], "seq", forward)
    high = lax.ppermute(value[:PAD], "seq", backward)
    return low, high


def exchange(blocks, bits=(4, 2, 1)):
    shape = blocks.shape
    cube = blocks.reshape((2, 2, 2) + shape[1:])
    for bit in bits:
        place = {4: 0, 2: 1, 1: 2}[bit]
        keep = lax.index_in_dim(cube, 0, place, keepdims=True)
        send = lax.index_in_dim(cube, 1, place, keepdims=True)
        cube = jnp.concatenate([keep, flip(send, "tp", bit)], axis=place)
    return cube.reshape(shape)


def gather_small(value, beside=()):
    blocks = value[None]
    for bit in (1, 2, 4):
        other = flip(blocks, "tp", bit)
        if bit == 4 and beside:
            other = after(other, *beside)
        blocks = jnp.concatenate([blocks, other], axis=0)
    return blocks


def sum_over_seq(value, bits=(1, 8, 2, 4)):
    for bit in bits:
        sent = value.astype(BF16)
        value = sent.astype(F32) + flip(sent, "seq", bit).astype(F32)
    return value


def gather_pieces(value):
    half = value.shape[0] // 2
    four = flip(value, "tp", 4)
    one = flip(value, "tp", 1)
    three = flip(value, "tp", 3)
    five = flip(four, "tp", 1)
    seven = flip(four, "tp", 3)
    two_a = flip(one[:half], "tp", 3)
    two_b = flip(three[half:], "tp", 1)
    six_a = flip(five[:half], "tp", 3)
    six_b = flip(seven[half:], "tp", 1)
    return value, one, three, four, five, seven, two_a, two_b, six_a, six_b


def hidden_logits_kernel(order, *refs):
    pieces = refs[:10]
    gen_ref, out_ref, edge_ref, flat_ref, tap_ref, full_ref, sems = refs[10:]
    members, rows, width = full_ref.shape
    half = rows // 2
    targets = [full_ref.at[order[at]] for at in (0, 1, 3, 4, 5, 7)]
    for at in (2, 6):
        targets.append(full_ref.at[order[at], 0:half])
        targets.append(full_ref.at[order[at], half:rows])
    copies = [
        pltpu.make_async_copy(ref, target, sems.at[index])
        for index, (ref, target) in enumerate(zip(pieces, targets))
    ]
    for copy in copies:
        copy.start()
    for copy in copies:
        copy.wait()
    backs = [
        pltpu.make_async_copy(full_ref.at[piece], out_ref.at[piece], sems.at[len(pieces) + piece])
        for piece in range(members)
    ]
    for copy in backs:
        copy.start()
    logits = jnp.zeros((gen_ref.shape[0], rows), F32)
    for piece in range(members):
        edge_ref[0, piece] = full_ref[piece, 0:PAD]
        edge_ref[1, piece] = full_ref[piece, rows - PAD :]
        logits = logits + lax.dot_general(
            gen_ref[:, piece * width : (piece + 1) * width],
            full_ref[piece],
            NT,
            preferred_element_type=F32,
        )
    exps = jnp.exp(logits)
    first = exps[0:KW]
    second = exps[KW : 2 * KW]
    first = first / jnp.sum(first, axis=0, keepdims=True)
    second = second / jnp.sum(second, axis=0, keepdims=True)
    blank = jnp.zeros((ROWS - 2 * KW, rows), F32)
    flat = jnp.concatenate([first, second, blank], axis=0)
    flat_ref[...] = flat
    tap_ref[...] = flat.T
    for copy in backs:
        copy.wait()


def hidden_logits(order, pieces, gen_rows):
    rows, width = pieces[0].shape
    columns, depth = gen_rows.shape
    members = depth // width
    whole = [pl.BlockSpec(memory_space=pltpu.HBM) for _ in pieces]
    return pl.pallas_call(
        hidden_logits_kernel,
        grid_spec=pltpu.PrefetchScalarGridSpec(
            num_scalar_prefetch=1,
            grid=(1,),
            in_specs=whole + [pl.BlockSpec((columns, depth), lambda i, o: (0, 0))],
            out_specs=[
                pl.BlockSpec(memory_space=pltpu.HBM),
                pl.BlockSpec((2, members, PAD, width), lambda i, o: (0, 0, 0, 0)),
                pl.BlockSpec((ROWS, rows), lambda i, o: (0, 0)),
                pl.BlockSpec((rows, ROWS), lambda i, o: (0, 0)),
            ],
            scratch_shapes=[
                pltpu.VMEM((members, rows, width), BF16),
                pltpu.SemaphoreType.DMA((len(pieces) + members,)),
            ],
        ),
        out_shape=(
            jax.ShapeDtypeStruct((members, rows, width), BF16),
            jax.ShapeDtypeStruct((2, members, PAD, width), BF16),
            jax.ShapeDtypeStruct((ROWS, rows), F32),
            jax.ShapeDtypeStruct((rows, ROWS), F32),
        ),
        compiler_params=params(),
        name="hidden_logits",
    )(order, *pieces, gen_rows)


def conv_up_kernel(
    order,
    hidden_ref,
    low_ref,
    high_ref,
    flat_one_ref,
    flat_two_ref,
    up_ref,
    grad_ref,
    act_ref,
    middle_ref,
    pre_grad_ref,
    padded,
    pre,
):
    count, rows, width = hidden_ref.shape
    step = 64
    reach = 2 * step
    heads = 2
    head_width = width // heads
    lane = lax.broadcasted_iota(jnp.int32, (step, reach), 1)
    term = None
    for piece, flat_ref in enumerate((flat_one_ref, flat_two_ref)):
        padded[piece, 0:PAD] = low_ref[piece]
        padded[piece, PAD : PAD + rows] = hidden_ref[piece]
        padded[piece, PAD + rows : 2 * PAD + rows] = high_ref[piece]
        padded[piece, 2 * PAD + rows :] = jnp.zeros((step - 2 * PAD, width), BF16)
        flat = flat_ref[0]
        taps = jnp.concatenate([flat, jnp.zeros((reach - ROWS, rows), F32)], axis=0).T
        for base in range(0, rows, step):
            for head in range(heads):
                lanes = slice(head * head_width, (head + 1) * head_width)
                mine = (lane >= head * KW) & (lane < (head + 1) * KW)
                own = jnp.where(mine, taps[base : base + step], 0.0)
                own = pltpu.roll(own, (1 - head * KW) % reach, 1)
                band = pltpu.roll(own, 0, 1, stride=1, stride_axis=0)
                upper = band.astype(BF16)
                lower = (band - upper.astype(F32)).astype(BF16)
                window = padded[piece, base : base + reach, lanes]
                both = jnp.dot(
                    jnp.concatenate([upper, lower], axis=0), window, preferred_element_type=F32
                )
                value = hidden_ref[piece, base : base + step, lanes].astype(F32)
                value = value + (both[:step] + both[step:])
                act_ref[piece, base : base + step, lanes] = value.astype(BF16)
        part = jnp.dot(
            act_ref[piece],
            up_ref[piece * width : (piece + 1) * width, :],
            preferred_element_type=F32,
        )
        term = part if term is None else term + part

    @pl.when(pl.program_id(0) == 0)
    def _():
        pre[...] = term

    @pl.when(pl.program_id(0) > 0)
    def _():
        pre[...] += term

    @pl.when(pl.program_id(0) == pl.num_programs(0) - 1)
    def _():
        scale = 0.7978845608028654
        chunk = 64

        def run(index, carry):
            at = pl.ds(pl.multiple_of(index * chunk, chunk), chunk)
            value = pre[at, :]
            square = value * value
            bent = jnp.tanh(scale * (value + 0.044715 * (square * value)))
            middle_ref[at, :] = (0.5 * value * (1.0 + bent)).astype(BF16)
            slope = 0.5 * (1.0 + bent) + 0.5 * value * (1.0 - bent * bent) * (
                scale * (1.0 + 3.0 * 0.044715 * square)
            )
            pre_grad_ref[at, :] = (grad_ref[at, :] * slope).astype(BF16)
            return carry

        lax.fori_loop(0, rows // chunk, run, 0)


def conv_up(order, hidden_full, low, high, flat_full, up_weight, middle_grad):
    members, rows, width = hidden_full.shape
    units = up_weight.shape[1]
    return pl.pallas_call(
        conv_up_kernel,
        grid_spec=pltpu.PrefetchScalarGridSpec(
            num_scalar_prefetch=1,
            grid=(members // 2,),
            in_specs=[
                pl.BlockSpec((2, rows, width), lambda i, o: (i, 0, 0)),
                pl.BlockSpec((2, PAD, width), lambda i, o: (i, 0, 0)),
                pl.BlockSpec((2, PAD, width), lambda i, o: (i, 0, 0)),
                pl.BlockSpec((1, ROWS, rows), lambda i, o: (o[2 * i], 0, 0)),
                pl.BlockSpec((1, ROWS, rows), lambda i, o: (o[2 * i + 1], 0, 0)),
                pl.BlockSpec((2 * width, units), lambda i, o: (i, 0)),
                pl.BlockSpec((rows, units), lambda i, o: (0, 0)),
            ],
            out_specs=[
                pl.BlockSpec((2, rows, width), lambda i, o: (i, 0, 0)),
                pl.BlockSpec((rows, units), lambda i, o: (0, 0)),
                pl.BlockSpec((rows, units), lambda i, o: (0, 0)),
            ],
            scratch_shapes=[
                pltpu.VMEM((2, rows + 64, width), BF16),
                pltpu.VMEM((rows, units), F32),
            ],
        ),
        out_shape=(
            jax.ShapeDtypeStruct((members, rows, width), BF16),
            jax.ShapeDtypeStruct((rows, units), BF16),
            jax.ShapeDtypeStruct((rows, units), BF16),
        ),
        compiler_params=params(),
        name="conv_up",
    )(order, hidden_full, low, high, flat_full, flat_full, up_weight, middle_grad)


def grad_middle_kernel(cot_ref, *refs):
    out_ref = refs[-1]
    width = cot_ref.shape[2]
    total = jnp.zeros(out_ref.shape, F32)
    for piece in range(cot_ref.shape[0]):
        ref = refs[piece // 2]
        lanes = slice(piece % 2 * width, (piece % 2 + 1) * width)
        total = total + lax.dot_general(
            cot_ref[piece], ref[:, lanes], NT, preferred_element_type=F32
        )
    out_ref[...] = total


def grad_middle(cot_full, down_weight):
    pieces, rows, width = cot_full.shape
    units = down_weight.shape[0]
    block = 256
    parts = pieces // 2
    return pl.pallas_call(
        grad_middle_kernel,
        grid=(units // block,),
        in_specs=[pl.BlockSpec((pieces, rows, width), lambda i: (0, 0, 0))]
        + [pl.BlockSpec((block, 2 * width), lambda i, q=q: (i, q)) for q in range(parts)],
        out_specs=pl.BlockSpec((rows, block), lambda i: (0, i)),
        out_shape=jax.ShapeDtypeStruct((rows, units), F32),
        compiler_params=params(),
        name="grad_middle",
    )(cot_full, *[down_weight] * parts)


def spread_kernel(transposed, order, value_ref, one_ref, two_ref, *out_refs):
    value = value_ref[...]
    if transposed:
        parts = [
            lax.dot_general(value, ref[...], NT, preferred_element_type=F32)
            for ref in (one_ref, two_ref)
        ]
        result = jnp.concatenate(parts, axis=1).astype(BF16)
    else:
        half = one_ref.shape[0]
        result = jnp.dot(value[:, :half], one_ref[...], preferred_element_type=F32)
        result = result + jnp.dot(value[:, half:], two_ref[...], preferred_element_type=F32)
        result = result.astype(BF16)
    for index, ref in enumerate(out_refs):

        @pl.when(lax.rem(pl.program_id(0), 4) == index)
        def _(ref=ref):
            ref[0] = result


def spread(order, value, weight, transposed, name, tokens=()):
    rows, units = value.shape
    if transposed:
        width = weight.shape[0] // 8
        block = (width // 2, units)
        specs = [
            pl.BlockSpec(block, lambda k, o: (2 * o[k], 0)),
            pl.BlockSpec(block, lambda k, o: (2 * o[k] + 1, 0)),
        ]
    else:
        width = weight.shape[1] // 8
        block = (units // 2, width)
        specs = [
            pl.BlockSpec(block, lambda k, o: (0, o[k])),
            pl.BlockSpec(block, lambda k, o: (1, o[k])),
        ]
    kernel, token_specs = ordered(functools.partial(spread_kernel, transposed), 4, tokens)
    return pl.pallas_call(
        kernel,
        grid_spec=pltpu.PrefetchScalarGridSpec(
            num_scalar_prefetch=1,
            grid=(8,),
            in_specs=[pl.BlockSpec((rows, units), lambda k, o: (0, 0))] + specs + token_specs,
            out_specs=[pl.BlockSpec((1, rows, width), lambda k, o: (k // 4, 0, 0))] * 4,
        ),
        out_shape=[jax.ShapeDtypeStruct((2, rows, width), BF16)] * 4,
        compiler_params=params(),
        name=name,
    )(order, value, weight, weight, *tokens)


def weight_grads_kernel(act_ref, cot_ref, pre_grad_ref, middle_ref, out_ref, held, sems):
    step = pl.program_id(0)
    last = pl.num_programs(0) - 1
    slot = lax.rem(step, 2)
    per = held.shape[1]
    chunk = held.shape[2] // 2

    def copies(at, place):
        return [
            pltpu.make_async_copy(
                held.at[place, index, part * chunk : (part + 1) * chunk],
                out_ref.at[per * at + index, part * chunk : (part + 1) * chunk],
                sems.at[place, 2 * index + part],
            )
            for index in range(per)
            for part in range(2)
        ]

    up = lax.dot_general(act_ref[0], pre_grad_ref[...], TN, preferred_element_type=F32)
    down = lax.dot_general(cot_ref[0], middle_ref[...], TN, preferred_element_type=F32)

    @pl.when(step >= 2)
    def _():
        for copy in copies(step - 2, slot):
            copy.wait()

    for index in range(per):
        rows = slice(index * chunk, (index + 1) * chunk)
        held[slot, index, 0:chunk] = up[rows].astype(BF16)
        held[slot, index, chunk:] = down[rows].astype(BF16)
    for copy in copies(step, slot):
        copy.start()

    @pl.when(step == last)
    def _():
        for copy in copies(step - 1, 1 - slot):
            copy.wait()
        for copy in copies(step, slot):
            copy.wait()


def weight_grads(act_full, cot_full, pre_grad, middle):
    pieces, rows, width = act_full.shape
    units = middle.shape[1]
    chunks = lax.axis_size("seq")
    per = chunks // pieces
    chunk = width // per
    return pl.pallas_call(
        weight_grads_kernel,
        grid=(pieces,),
        in_specs=[
            pl.BlockSpec((1, rows, width), lambda i: (i, 0, 0)),
            pl.BlockSpec((1, rows, width), lambda i: (i, 0, 0)),
            pl.BlockSpec((rows, units), lambda i: (0, 0)),
            pl.BlockSpec((rows, units), lambda i: (0, 0)),
        ],
        out_specs=pl.BlockSpec(memory_space=pltpu.HBM),
        out_shape=jax.ShapeDtypeStruct((chunks, 2 * chunk, units), BF16),
        scratch_shapes=[
            pltpu.VMEM((2, per, 2 * chunk, units), BF16),
            pltpu.SemaphoreType.DMA((2, 2 * per)),
        ],
        compiler_params=params(),
        name="weight_grads",
    )(act_full, cot_full, pre_grad, middle)


def kernel_grad_kernel(*refs):
    terms = refs[:5]
    cot_ref, hidden_ref, low_ref, high_ref, tap_ref = refs[5:10]
    grad_ref, logit_ref, padded, found_ref = refs[10:]
    rows, width = hidden_ref.shape
    heads = 2
    head_width = width // heads
    padded[0:PAD] = low_ref[...].astype(F32)
    padded[PAD : PAD + rows] = hidden_ref[...].astype(F32)
    padded[PAD + rows :] = high_ref[...].astype(F32)
    step = 32
    lane = lax.broadcasted_iota(jnp.int32, (step, ROWS), 1)

    def run(index, carry):
        base = pl.multiple_of(index * step, step)
        at = pl.ds(base, step)
        grad = terms[0][at, :].astype(F32)
        for ref in terms[1:]:
            grad = grad + ref[at, :].astype(F32)
        grad = grad + cot_ref[at, :].astype(F32)
        grad_ref[at, :] = grad
        taps = tap_ref[at, :]
        found = jnp.zeros((step, ROWS), F32)
        for head in range(heads):
            lanes = slice(head * head_width, (head + 1) * head_width)
            window = padded[pl.ds(base, step + 2 * PAD), lanes]
            part = grad[:, lanes]
            for tap in range(KW):
                column = head * KW + tap
                value = jnp.sum(part * window[tap + 1 : tap + 1 + step], axis=1, keepdims=True)
                found = jnp.where(lane == column, value, found)
        product = taps * found
        in_first = lane < KW
        one = jnp.sum(jnp.where(in_first, product, 0.0), axis=1, keepdims=True)
        two = jnp.sum(jnp.where(in_first, 0.0, product), axis=1, keepdims=True)
        found_ref[at, :] = taps * (found - jnp.where(in_first, one, two))
        return carry

    lax.fori_loop(0, rows // step, run, 0)
    logit_ref[...] = found_ref[...].T.astype(BF16)


def kernel_grads(pairs, last, cotangent, hidden, low, high, taps, tokens):
    rows, width = hidden.shape
    flat = pl.BlockSpec((rows, width), lambda i: (0, 0))
    edge = pl.BlockSpec((PAD, width), lambda i: (0, 0))
    kernel, token_specs = ordered(kernel_grad_kernel, 10, tokens)
    return pl.pallas_call(
        kernel,
        grid=(1,),
        in_specs=[pl.BlockSpec((None, rows, width), lambda i: (0, 0, 0))] * 4
        + [flat, flat, flat, edge, edge, pl.BlockSpec((rows, ROWS), lambda i: (0, 0))]
        + token_specs,
        out_specs=[flat, pl.BlockSpec((ROWS, rows), lambda i: (0, 0))],
        out_shape=(
            jax.ShapeDtypeStruct((rows, width), F32),
            jax.ShapeDtypeStruct((ROWS, rows), BF16),
        ),
        scratch_shapes=[
            pltpu.VMEM((rows + 2 * PAD, width), F32),
            pltpu.VMEM((rows, ROWS), F32),
        ],
        compiler_params=params(24),
        name="kernel_grads",
    )(*pairs, last, cotangent, hidden, low, high, taps, *tokens)


def hidden_grad_kernel(
    grad_ref,
    glow_ref,
    ghigh_ref,
    tap_ref,
    tlow_ref,
    thigh_ref,
    logit_ref,
    gen_ref,
    mask_ref,
    code_ref,
    embed_ref,
    table_ref,
    padded,
    tapped,
    back,
):
    rows, width = grad_ref.shape
    heads = 2
    head_width = width // heads
    padded[0:PAD] = glow_ref[...].astype(F32)
    padded[PAD : PAD + rows] = grad_ref[...]
    padded[PAD + rows :] = ghigh_ref[...].astype(F32)
    tapped[0:PAD] = tlow_ref[...]
    tapped[PAD : PAD + rows] = tap_ref[...]
    tapped[PAD + rows :] = thigh_ref[...]
    back[...] = lax.dot_general(logit_ref[...], gen_ref[...], TN, preferred_element_type=F32)
    step = 32

    def run(index, carry):
        base = pl.multiple_of(index * step, step)
        at = pl.ds(base, step)
        picked = mask_ref[at, :] == 1
        taps = tapped[pl.ds(base, step + 2 * PAD), :]
        for head in range(heads):
            lanes = slice(head * head_width, (head + 1) * head_width)
            window = padded[pl.ds(base, step + 2 * PAD), lanes]
            total = window[PAD : PAD + step] + back[at, lanes]
            for tap in range(KW):
                column = head * KW + tap
                lower = 2 * PAD - 1 - tap
                total = (
                    total
                    + taps[lower : lower + step, column : column + 1]
                    * window[lower : lower + step]
                )
            embed_ref[at, lanes] = jnp.where(picked, 0.0, total)
            back[at, lanes] = jnp.where(picked, total, 0.0)
        return carry

    lax.fori_loop(0, rows // step, run, 0)
    codes = lax.broadcasted_iota(jnp.int32, (table_ref.shape[0], rows), 0)
    chosen = jnp.where(codes == code_ref[...], 1.0, 0.0).astype(BF16)
    value = back[...]
    upper = value.astype(BF16)
    lower = (value - upper.astype(F32)).astype(BF16)
    table_ref[...] = jnp.dot(chosen, upper, preferred_element_type=F32) + jnp.dot(
        chosen, lower, preferred_element_type=F32
    )


def hidden_grads(operands, codes, tokens):
    rows, width = operands[0].shape
    kernel, token_specs = ordered(hidden_grad_kernel, len(operands), tokens)
    whole = [pl.BlockSpec(o.shape, lambda i: (0, 0)) for o in operands]
    return pl.pallas_call(
        kernel,
        grid=(1,),
        in_specs=whole + token_specs,
        out_specs=[
            pl.BlockSpec((rows, width), lambda i: (0, 0)),
            pl.BlockSpec((codes, width), lambda i: (0, 0)),
        ],
        out_shape=(
            jax.ShapeDtypeStruct((rows, width), F32),
            jax.ShapeDtypeStruct((codes, width), F32),
        ),
        scratch_shapes=[
            pltpu.VMEM((rows + 2 * PAD, width), F32),
            pltpu.VMEM((rows + 2 * PAD, ROWS), F32),
            pltpu.VMEM((rows, width), F32),
        ],
        compiler_params=params(24),
        name="hidden_grads",
    )(*operands, *tokens)


def gen_blocks_kernel(order, gen_ref, token_ref, out_ref):
    columns = gen_ref.shape[0]
    members, _, width = out_ref.shape
    out_ref[...] = jnp.zeros_like(out_ref)
    for k in range(members):
        at = pl.multiple_of(order[k] * width, width)
        out_ref[k, 0:columns] = gen_ref[:, pl.ds(at, width)]


def gen_blocks(order, gen_rows, width, token):
    columns, depth = gen_rows.shape
    members = depth // width
    return pl.pallas_call(
        gen_blocks_kernel,
        grid_spec=pltpu.PrefetchScalarGridSpec(
            num_scalar_prefetch=1,
            grid=(1,),
            in_specs=[
                pl.BlockSpec((columns, depth), lambda i, o: (0, 0)),
                pl.BlockSpec(memory_space=pl.ANY),
            ],
            out_specs=pl.BlockSpec((members, ROWS, width), lambda i, o: (0, 0, 0)),
        ),
        out_shape=jax.ShapeDtypeStruct((members, ROWS, width), BF16),
        compiler_params=params(24),
        name="gen_blocks",
    )(order, gen_rows, token)


def gen_grads_kernel(logit_ref, hidden_ref, out_ref):
    width = hidden_ref.shape[2]
    for piece in range(hidden_ref.shape[0]):
        out_ref[:, piece * width : (piece + 1) * width] = jnp.dot(
            logit_ref[...], hidden_ref[piece], preferred_element_type=F32
        )


def gen_grads(logit_grad, hidden_full):
    members, rows, width = hidden_full.shape
    heads = logit_grad.shape[0]
    return pl.pallas_call(
        gen_grads_kernel,
        out_shape=jax.ShapeDtypeStruct((heads, members * width), F32),
        compiler_params=params(24),
        name="gen_grads",
    )(logit_grad, hidden_full)


def add_up(values):
    total = values[0].astype(F32)
    for value in values[1:]:
        total = total + value.astype(F32)
    return total


def swap_pairs(pairs):
    return [pairs[0]] + [flip(pairs[z], "tp", z) for z in (1, 2, 3)]


def body(
    embeddings,
    span_mask,
    sentinel_id,
    sentinel_table,
    gen_weight,
    up_weight,
    down_weight,
    cotangent,
):
    rows, width = embeddings.shape
    codes = sentinel_table.shape[0]
    members = lax.axis_size("tp")
    me = lax.axis_index("tp")
    order = jnp.arange(members, dtype=jnp.int32) ^ me.astype(jnp.int32)

    sentinel_codes = jnp.arange(codes, dtype=jnp.int32)
    onehot = (sentinel_id[:, None] == sentinel_codes[None, :]).astype(BF16)
    picked = jnp.dot(onehot, sentinel_table, preferred_element_type=F32).astype(BF16)
    hidden = jnp.where(span_mask[:, None] == 1, picked, embeddings)
    pieces = gather_pieces(hidden)
    cot_full = lax.all_gather(cotangent, "tp", axis=0, tiled=False)

    hidden_full, edges, flat, taps = hidden_logits(order, pieces, gen_weight.T)
    high_full, low_full = edges[0], edges[1]
    count = lax.axis_size("seq")
    low_full = lax.ppermute(low_full, "seq", [(i, i + 1) for i in range(count - 1)])
    high_full = lax.ppermute(high_full, "seq", [(i + 1, i) for i in range(count - 1)])
    middle_grad = grad_middle(cot_full, down_weight)
    flat_full = gather_small(flat, (middle_grad,))
    act_full, middle, pre_grad = conv_up(
        order, hidden_full, low_full, high_full, flat_full, up_weight, middle_grad
    )

    summed = weight_grads(act_full, cot_full, pre_grad, middle)
    back_own = spread(order, pre_grad, up_weight, True, "act_back", (summed,))
    back_pairs = swap_pairs(back_own)
    summed = lax.psum_scatter(summed, "seq", scatter_dimension=0, tiled=False)

    columns = gen_weight.shape[1]
    gen_full = gen_blocks(order, gen_weight.T, width, back_own[0])
    gen_full = exchange(gen_full, (4,))
    out_pairs = swap_pairs(spread(order, middle, down_weight, False, "ffn_out", (gen_full,)))
    gen_full = exchange(gen_full, (2, 1)).reshape(members * ROWS, width)
    tap_low, tap_high = halo(taps)

    out_last = flip(add_up([pair[1] for pair in out_pairs]).astype(BF16), "tp", 4)
    back_last = flip(add_up([pair[1] for pair in back_pairs]).astype(BF16), "tp", 4)
    low = lax.dynamic_index_in_dim(low_full, me, 0, keepdims=False)
    high = lax.dynamic_index_in_dim(high_full, me, 0, keepdims=False)
    grad, logit_grad = kernel_grads(
        back_pairs,
        back_last,
        cotangent,
        hidden,
        low,
        high,
        taps,
        (gen_full, tap_low, tap_high),
    )
    grad_low, grad_high = halo(grad.astype(BF16))
    logit_full = gather_small(logit_grad).reshape(members * ROWS, rows)
    gen_sum = sum_over_seq(gen_grads(logit_grad, hidden_full), (1, 8))
    embed_grad, table_part = hidden_grads(
        (
            grad,
            grad_low,
            grad_high,
            taps,
            tap_low,
            tap_high,
            logit_full,
            gen_full,
            span_mask[:, None],
            sentinel_id[None, :],
        ),
        codes,
        (gen_sum, out_last),
    )
    gen_sum = sum_over_seq(gen_sum, (2, 4))
    gen_grad = gen_sum[:columns].T
    table_grad = sum_over_seq(table_part)

    total = add_up([pair[0] for pair in out_pairs] + [out_last])
    act = lax.dynamic_index_in_dim(act_full, me, 0, keepdims=False)
    layer_output = (act.astype(F32) + total).astype(BF16)

    chunk = summed.shape[0] // 2
    up_grad = summed[:chunk].astype(F32)
    down_grad = summed[chunk:].astype(F32).T
    return (layer_output, embed_grad, table_grad, gen_grad, up_grad, down_grad)


def solution(mesh):
    placed = (
        P("seq", "tp"),
        P("seq"),
        P("seq"),
        P(None, "tp"),
        P(None, "tp"),
        P(None, "tp"),
        P("tp", None),
        P("seq", "tp"),
    )
    return jax.shard_map(
        body,
        mesh=mesh,
        in_specs=placed,
        out_specs=(
            P("seq", "tp"),
            P("seq", "tp"),
            P(None, "tp"),
            P(None, "tp"),
            P("seq", "tp"),
            P("tp", "seq"),
        ),
        check_vma=False,
    )
```

```python
import functools

import jax
import jax.numpy as jnp
from jax import lax
from jax.experimental import pallas as pl
from jax.experimental.pallas import tpu as pltpu
from jax.sharding import PartitionSpec as P

KW = 15
REACH = 7
PAD = 8
ROWS = 32
F32 = jnp.float32
BF16 = jnp.bfloat16
NT = (((1,), (1,)), ((), ()))
TN = (((0,), (0,)), ((), ()))


def params(megabytes=60):
    return pltpu.CompilerParams(vmem_limit_bytes=megabytes << 20)


def after(value, *others):
    return lax.optimization_barrier((value, *others))[0]


def ordered(kernel, inputs, tokens):
    def run(*refs):
        kernel(*refs[:inputs], *refs[inputs + len(tokens) :])

    return run, [pl.BlockSpec(memory_space=pltpu.HBM) for _ in tokens]


def flip(value, axis, bit):
    count = lax.axis_size(axis)
    return lax.ppermute(value, axis, [(i, i ^ bit) for i in range(count)])


def halo(value):
    count = lax.axis_size("seq")
    forward = [(i, i + 1) for i in range(count - 1)]
    backward = [(i + 1, i) for i in range(count - 1)]
    low = lax.ppermute(value[-PAD:], "seq", forward)
    high = lax.ppermute(value[:PAD], "seq", backward)
    return low, high


def exchange(blocks, bits=(4, 2, 1)):
    shape = blocks.shape
    cube = blocks.reshape((2, 2, 2) + shape[1:])
    for bit in bits:
        place = {4: 0, 2: 1, 1: 2}[bit]
        keep = lax.index_in_dim(cube, 0, place, keepdims=True)
        send = lax.index_in_dim(cube, 1, place, keepdims=True)
        cube = jnp.concatenate([keep, flip(send, "tp", bit)], axis=place)
    return cube.reshape(shape)


def gather_small(value, beside=()):
    blocks = value[None]
    for bit in (1, 2, 4):
        other = flip(blocks, "tp", bit)
        if bit == 4 and beside:
            other = after(other, *beside)
        blocks = jnp.concatenate([blocks, other], axis=0)
    return blocks


def sum_over_seq(value, bits=(1, 8, 2, 4)):
    for bit in bits:
        sent = value.astype(BF16)
        value = sent.astype(F32) + flip(sent, "seq", bit).astype(F32)
    return value


def gather_pieces(value):
    half = value.shape[0] // 2
    four = flip(value, "tp", 4)
    one = flip(value, "tp", 1)
    three = flip(value, "tp", 3)
    five = flip(four, "tp", 1)
    seven = flip(four, "tp", 3)
    two_a = flip(one[:half], "tp", 3)
    two_b = flip(three[half:], "tp", 1)
    six_a = flip(five[:half], "tp", 3)
    six_b = flip(seven[half:], "tp", 1)
    return value, one, three, four, five, seven, two_a, two_b, six_a, six_b


def hidden_logits_kernel(order, *refs):
    pieces = refs[:10]
    gen_ref, out_ref, edge_ref, flat_ref, tap_ref, full_ref, sems = refs[10:]
    members, rows, width = full_ref.shape
    half = rows // 2
    targets = [full_ref.at[order[at]] for at in (0, 1, 3, 4, 5, 7)]
    for at in (2, 6):
        targets.append(full_ref.at[order[at], 0:half])
        targets.append(full_ref.at[order[at], half:rows])
    copies = [
        pltpu.make_async_copy(ref, target, sems.at[index])
        for index, (ref, target) in enumerate(zip(pieces, targets))
    ]
    for copy in copies:
        copy.start()
    for copy in copies:
        copy.wait()
    backs = [
        pltpu.make_async_copy(full_ref.at[piece], out_ref.at[piece], sems.at[len(pieces) + piece])
        for piece in range(members)
    ]
    for copy in backs:
        copy.start()
    logits = jnp.zeros((gen_ref.shape[0], rows), F32)
    for piece in range(members):
        edge_ref[0, piece] = full_ref[piece, 0:PAD]
        edge_ref[1, piece] = full_ref[piece, rows - PAD :]
        logits = logits + lax.dot_general(
            gen_ref[:, piece * width : (piece + 1) * width],
            full_ref[piece],
            NT,
            preferred_element_type=F32,
        )
    exps = jnp.exp(logits)
    first = exps[0:KW]
    second = exps[KW : 2 * KW]
    first = first / jnp.sum(first, axis=0, keepdims=True)
    second = second / jnp.sum(second, axis=0, keepdims=True)
    blank = jnp.zeros((ROWS - 2 * KW, rows), F32)
    flat = jnp.concatenate([first, second, blank], axis=0)
    flat_ref[...] = flat
    tap_ref[...] = flat.T
    for copy in backs:
        copy.wait()


def hidden_logits(order, pieces, gen_rows):
    rows, width = pieces[0].shape
    columns, depth = gen_rows.shape
    members = depth // width
    whole = [pl.BlockSpec(memory_space=pltpu.HBM) for _ in pieces]
    return pl.pallas_call(
        hidden_logits_kernel,
        grid_spec=pltpu.PrefetchScalarGridSpec(
            num_scalar_prefetch=1,
            grid=(1,),
            in_specs=whole + [pl.BlockSpec((columns, depth), lambda i, o: (0, 0))],
            out_specs=[
                pl.BlockSpec(memory_space=pltpu.HBM),
                pl.BlockSpec((2, members, PAD, width), lambda i, o: (0, 0, 0, 0)),
                pl.BlockSpec((ROWS, rows), lambda i, o: (0, 0)),
                pl.BlockSpec((rows, ROWS), lambda i, o: (0, 0)),
            ],
            scratch_shapes=[
                pltpu.VMEM((members, rows, width), BF16),
                pltpu.SemaphoreType.DMA((len(pieces) + members,)),
            ],
        ),
        out_shape=(
            jax.ShapeDtypeStruct((members, rows, width), BF16),
            jax.ShapeDtypeStruct((2, members, PAD, width), BF16),
            jax.ShapeDtypeStruct((ROWS, rows), F32),
            jax.ShapeDtypeStruct((rows, ROWS), F32),
        ),
        compiler_params=params(),
        name="hidden_logits",
    )(order, *pieces, gen_rows)


def layer_kernel(
    order,
    hidden_ref,
    low_ref,
    high_ref,
    flat_one_ref,
    flat_two_ref,
    up_ref,
    grad_ref,
    cot_ref,
    summed_ref,
    own_ref,
    middle_ref,
    zero_ref,
    one_ref,
    two_ref,
    three_ref,
    padded,
    pre,
    pre_grad,
    act,
    up_kept,
    held,
    sems,
):
    index = pl.program_id(0)
    count, rows, width = hidden_ref.shape
    firsts = act.shape[0] // count

    @pl.when(index < firsts)
    def _():
        step = 64
        reach = 2 * step
        heads = 2
        head_width = width // heads
        lane = lax.broadcasted_iota(jnp.int32, (step, reach), 1)
        depth = up_ref.shape[0]
        up_kept[pl.ds(pl.multiple_of(index * depth, depth), depth)] = up_ref[...]
        term = None
        for piece, flat_ref in enumerate((flat_one_ref, flat_two_ref)):
            at = count * index + piece
            padded[piece, 0:PAD] = low_ref[piece]
            padded[piece, PAD : PAD + rows] = hidden_ref[piece]
            padded[piece, PAD + rows : 2 * PAD + rows] = high_ref[piece]
            padded[piece, 2 * PAD + rows :] = jnp.zeros((step - 2 * PAD, width), BF16)
            flat = flat_ref[0]
            taps = jnp.concatenate([flat, jnp.zeros((reach - ROWS, rows), F32)], axis=0).T
            for base in range(0, rows, step):
                for head in range(heads):
                    lanes = slice(head * head_width, (head + 1) * head_width)
                    mine = (lane >= head * KW) & (lane < (head + 1) * KW)
                    own = jnp.where(mine, taps[base : base + step], 0.0)
                    own = pltpu.roll(own, (1 - head * KW) % reach, 1)
                    band = pltpu.roll(own, 0, 1, stride=1, stride_axis=0)
                    upper = band.astype(BF16)
                    lower = (band - upper.astype(F32)).astype(BF16)
                    window = padded[piece, base : base + reach, lanes]
                    both = jnp.dot(
                        jnp.concatenate([upper, lower], axis=0),
                        window,
                        preferred_element_type=F32,
                    )
                    value = hidden_ref[piece, base : base + step, lanes].astype(F32)
                    value = value + (both[:step] + both[step:])
                    act[at, base : base + step, lanes] = value.astype(BF16)
            part = jnp.dot(
                act[at],
                up_ref[piece * width : (piece + 1) * width, :],
                preferred_element_type=F32,
            )
            term = part if term is None else term + part

        @pl.when(index == 0)
        def _():
            pre[...] = term

        @pl.when(index > 0)
        def _():
            pre[...] += term

    @pl.when(index == firsts - 1)
    def _():
        scale = 0.7978845608028654
        chunk = 64

        def run(turn, carry):
            at = pl.ds(pl.multiple_of(turn * chunk, chunk), chunk)
            value = pre[at, :]
            square = value * value
            bent = jnp.tanh(scale * (value + 0.044715 * (square * value)))
            middle_ref[at, :] = (0.5 * value * (1.0 + bent)).astype(BF16)
            slope = 0.5 * (1.0 + bent) + 0.5 * value * (1.0 - bent * bent) * (
                scale * (1.0 + 3.0 * 0.044715 * square)
            )
            pre_grad[at, :] = (grad_ref[at, :] * slope).astype(BF16)
            return carry

        lax.fori_loop(0, rows // chunk, run, 0)
        own_ref[...] = act[order[0]]

    turn = index - firsts
    last = act.shape[0] - 1
    per = held.shape[1]
    half = held.shape[2] // 2

    def copies(at, slot):
        return [
            pltpu.make_async_copy(
                held.at[slot, chunk, part * half : (part + 1) * half],
                summed_ref.at[per * at + chunk, part * half : (part + 1) * half],
                sems.at[slot, 2 * chunk + part],
            )
            for chunk in range(per)
            for part in range(2)
        ]

    @pl.when(turn >= 0)
    def _():
        slot = lax.rem(turn, 2)
        up = lax.dot_general(act[turn], pre_grad[...], TN, preferred_element_type=F32)
        down = lax.dot_general(cot_ref[0], middle_ref[...], TN, preferred_element_type=F32)

        @pl.when(turn >= 2)
        def _():
            for copy in copies(turn - 2, slot):
                copy.wait()

        for chunk in range(per):
            lines = slice(chunk * half, (chunk + 1) * half)
            held[slot, chunk, 0:half] = up[lines].astype(BF16)
            held[slot, chunk, half:] = down[lines].astype(BF16)
        for copy in copies(turn, slot):
            copy.start()
        at = pl.multiple_of(order[turn] * width, width)
        result = lax.dot_general(
            pre_grad[...], up_kept[pl.ds(at, width)], NT, preferred_element_type=F32
        ).astype(BF16)
        for z, ref in enumerate((zero_ref, one_ref, two_ref, three_ref)):

            @pl.when(lax.rem(turn, 4) == z)
            def _(ref=ref):
                ref[0] = result

        @pl.when(turn == last)
        def _():
            for copy in copies(turn - 1, 1 - slot):
                copy.wait()
            for copy in copies(turn, slot):
                copy.wait()


def layer(order, hidden_full, low, high, flat_full, up_weight, middle_grad, cot_full, tokens):
    members, rows, width = hidden_full.shape
    units = up_weight.shape[1]
    firsts = members // 2
    chunks = lax.axis_size("seq")
    per = chunks // members
    chunk = width // per
    kernel, token_specs = ordered(layer_kernel, 9, tokens)

    def pair(i):
        return jnp.minimum(i, firsts - 1)

    def turn(i):
        return jnp.maximum(i - firsts, 0)

    return pl.pallas_call(
        kernel,
        grid_spec=pltpu.PrefetchScalarGridSpec(
            num_scalar_prefetch=1,
            grid=(firsts + members,),
            in_specs=[
                pl.BlockSpec((2, rows, width), lambda i, o: (pair(i), 0, 0)),
                pl.BlockSpec((2, PAD, width), lambda i, o: (pair(i), 0, 0)),
                pl.BlockSpec((2, PAD, width), lambda i, o: (pair(i), 0, 0)),
                pl.BlockSpec((1, ROWS, rows), lambda i, o: (o[2 * pair(i)], 0, 0)),
                pl.BlockSpec((1, ROWS, rows), lambda i, o: (o[2 * pair(i) + 1], 0, 0)),
                pl.BlockSpec((2 * width, units), lambda i, o: (pair(i), 0)),
                pl.BlockSpec((rows, units), lambda i, o: (0, 0)),
                pl.BlockSpec((1, rows, width), lambda i, o: (turn(i), 0, 0)),
            ]
            + token_specs,
            out_specs=[
                pl.BlockSpec(memory_space=pltpu.HBM),
                pl.BlockSpec((rows, width), lambda i, o: (0, 0)),
                pl.BlockSpec((rows, units), lambda i, o: (0, 0)),
            ]
            + [pl.BlockSpec((1, rows, width), lambda i, o: (turn(i) // 4, 0, 0))] * 4,
            scratch_shapes=[
                pltpu.VMEM((2, rows + 64, width), BF16),
                pltpu.VMEM((rows, units), F32),
                pltpu.VMEM((rows, units), BF16),
                pltpu.VMEM((members, rows, width), BF16),
                pltpu.VMEM((members * width, units), BF16),
                pltpu.VMEM((2, per, 2 * chunk, units), BF16),
                pltpu.SemaphoreType.DMA((2, 2 * per)),
            ],
        ),
        out_shape=[
            jax.ShapeDtypeStruct((chunks, 2 * chunk, units), BF16),
            jax.ShapeDtypeStruct((rows, width), BF16),
            jax.ShapeDtypeStruct((rows, units), BF16),
        ]
        + [jax.ShapeDtypeStruct((2, rows, width), BF16)] * 4,
        compiler_params=params(),
        name="layer",
    )(
        order,
        hidden_full,
        low,
        high,
        flat_full,
        flat_full,
        up_weight,
        middle_grad,
        cot_full,
        *tokens,
    )


def grad_middle_kernel(cot_ref, *refs):
    out_ref = refs[-1]
    width = cot_ref.shape[2]
    total = jnp.zeros(out_ref.shape, F32)
    for piece in range(cot_ref.shape[0]):
        ref = refs[piece // 2]
        lanes = slice(piece % 2 * width, (piece % 2 + 1) * width)
        total = total + lax.dot_general(
            cot_ref[piece], ref[:, lanes], NT, preferred_element_type=F32
        )
    out_ref[...] = total


def grad_middle(cot_full, down_weight):
    pieces, rows, width = cot_full.shape
    units = down_weight.shape[0]
    block = 256
    parts = pieces // 2
    return pl.pallas_call(
        grad_middle_kernel,
        grid=(units // block,),
        in_specs=[pl.BlockSpec((pieces, rows, width), lambda i: (0, 0, 0))]
        + [pl.BlockSpec((block, 2 * width), lambda i, q=q: (i, q)) for q in range(parts)],
        out_specs=pl.BlockSpec((rows, block), lambda i: (0, i)),
        out_shape=jax.ShapeDtypeStruct((rows, units), F32),
        compiler_params=params(),
        name="grad_middle",
    )(cot_full, *[down_weight] * parts)


def spread_kernel(order, value_ref, weight_ref, *out_refs):
    result = jnp.dot(value_ref[...], weight_ref[...], preferred_element_type=F32).astype(BF16)
    for index, ref in enumerate(out_refs):

        @pl.when(lax.rem(pl.program_id(0), 4) == index)
        def _(ref=ref):
            ref[0] = result


def spread(order, value, weight, tokens):
    rows, units = value.shape
    width = weight.shape[1] // 8
    kernel, token_specs = ordered(spread_kernel, 3, tokens)
    return pl.pallas_call(
        kernel,
        grid_spec=pltpu.PrefetchScalarGridSpec(
            num_scalar_prefetch=1,
            grid=(8,),
            in_specs=[
                pl.BlockSpec((rows, units), lambda k, o: (0, 0)),
                pl.BlockSpec((units, width), lambda k, o: (0, o[k])),
            ]
            + token_specs,
            out_specs=[pl.BlockSpec((1, rows, width), lambda k, o: (k // 4, 0, 0))] * 4,
        ),
        out_shape=[jax.ShapeDtypeStruct((2, rows, width), BF16)] * 4,
        compiler_params=params(),
        name="ffn_out",
    )(order, value, weight, *tokens)


def kernel_grad_kernel(*refs):
    terms = refs[:5]
    cot_ref, hidden_ref, low_ref, high_ref, tap_ref = refs[5:10]
    grad_ref, logit_ref, padded, found_ref = refs[10:]
    rows, width = hidden_ref.shape
    heads = 2
    head_width = width // heads
    padded[0:PAD] = low_ref[...].astype(F32)
    padded[PAD : PAD + rows] = hidden_ref[...].astype(F32)
    padded[PAD + rows :] = high_ref[...].astype(F32)
    step = 32
    lane = lax.broadcasted_iota(jnp.int32, (step, ROWS), 1)

    def run(index, carry):
        base = pl.multiple_of(index * step, step)
        at = pl.ds(base, step)
        grad = terms[0][at, :].astype(F32)
        for ref in terms[1:]:
            grad = grad + ref[at, :].astype(F32)
        grad = grad + cot_ref[at, :].astype(F32)
        grad_ref[at, :] = grad
        taps = tap_ref[at, :]
        found = jnp.zeros((step, ROWS), F32)
        for head in range(heads):
            lanes = slice(head * head_width, (head + 1) * head_width)
            window = padded[pl.ds(base, step + 2 * PAD), lanes]
            part = grad[:, lanes]
            for tap in range(KW):
                column = head * KW + tap
                value = jnp.sum(part * window[tap + 1 : tap + 1 + step], axis=1, keepdims=True)
                found = jnp.where(lane == column, value, found)
        product = taps * found
        in_first = lane < KW
        one = jnp.sum(jnp.where(in_first, product, 0.0), axis=1, keepdims=True)
        two = jnp.sum(jnp.where(in_first, 0.0, product), axis=1, keepdims=True)
        found_ref[at, :] = taps * (found - jnp.where(in_first, one, two))
        return carry

    lax.fori_loop(0, rows // step, run, 0)
    logit_ref[...] = found_ref[...].T.astype(BF16)


def kernel_grads(pairs, last, cotangent, hidden, low, high, taps, tokens):
    rows, width = hidden.shape
    flat = pl.BlockSpec((rows, width), lambda i: (0, 0))
    edge = pl.BlockSpec((PAD, width), lambda i: (0, 0))
    kernel, token_specs = ordered(kernel_grad_kernel, 10, tokens)
    return pl.pallas_call(
        kernel,
        grid=(1,),
        in_specs=[pl.BlockSpec((None, rows, width), lambda i: (0, 0, 0))] * 4
        + [flat, flat, flat, edge, edge, pl.BlockSpec((rows, ROWS), lambda i: (0, 0))]
        + token_specs,
        out_specs=[flat, pl.BlockSpec((ROWS, rows), lambda i: (0, 0))],
        out_shape=(
            jax.ShapeDtypeStruct((rows, width), F32),
            jax.ShapeDtypeStruct((ROWS, rows), BF16),
        ),
        scratch_shapes=[
            pltpu.VMEM((rows + 2 * PAD, width), F32),
            pltpu.VMEM((rows, ROWS), F32),
        ],
        compiler_params=params(24),
        name="kernel_grads",
    )(*pairs, last, cotangent, hidden, low, high, taps, *tokens)


def hidden_grad_kernel(
    grad_ref,
    glow_ref,
    ghigh_ref,
    tap_ref,
    tlow_ref,
    thigh_ref,
    logit_ref,
    gen_ref,
    mask_ref,
    code_ref,
    embed_ref,
    table_ref,
    padded,
    tapped,
    back,
):
    rows, width = grad_ref.shape
    heads = 2
    head_width = width // heads
    padded[0:PAD] = glow_ref[...].astype(F32)
    padded[PAD : PAD + rows] = grad_ref[...]
    padded[PAD + rows :] = ghigh_ref[...].astype(F32)
    tapped[0:PAD] = tlow_ref[...]
    tapped[PAD : PAD + rows] = tap_ref[...]
    tapped[PAD + rows :] = thigh_ref[...]
    back[...] = lax.dot_general(logit_ref[...], gen_ref[...], TN, preferred_element_type=F32)
    step = 32

    def run(index, carry):
        base = pl.multiple_of(index * step, step)
        at = pl.ds(base, step)
        picked = mask_ref[at, :] == 1
        taps = tapped[pl.ds(base, step + 2 * PAD), :]
        for head in range(heads):
            lanes = slice(head * head_width, (head + 1) * head_width)
            window = padded[pl.ds(base, step + 2 * PAD), lanes]
            total = window[PAD : PAD + step] + back[at, lanes]
            for tap in range(KW):
                column = head * KW + tap
                lower = 2 * PAD - 1 - tap
                total = (
                    total
                    + taps[lower : lower + step, column : column + 1]
                    * window[lower : lower + step]
                )
            embed_ref[at, lanes] = jnp.where(picked, 0.0, total)
            back[at, lanes] = jnp.where(picked, total, 0.0)
        return carry

    lax.fori_loop(0, rows // step, run, 0)
    codes = lax.broadcasted_iota(jnp.int32, (table_ref.shape[0], rows), 0)
    chosen = jnp.where(codes == code_ref[...], 1.0, 0.0).astype(BF16)
    value = back[...]
    upper = value.astype(BF16)
    lower = (value - upper.astype(F32)).astype(BF16)
    table_ref[...] = jnp.dot(chosen, upper, preferred_element_type=F32) + jnp.dot(
        chosen, lower, preferred_element_type=F32
    )


def hidden_grads(operands, codes, tokens):
    rows, width = operands[0].shape
    kernel, token_specs = ordered(hidden_grad_kernel, len(operands), tokens)
    whole = [pl.BlockSpec(o.shape, lambda i: (0, 0)) for o in operands]
    return pl.pallas_call(
        kernel,
        grid=(1,),
        in_specs=whole + token_specs,
        out_specs=[
            pl.BlockSpec((rows, width), lambda i: (0, 0)),
            pl.BlockSpec((codes, width), lambda i: (0, 0)),
        ],
        out_shape=(
            jax.ShapeDtypeStruct((rows, width), F32),
            jax.ShapeDtypeStruct((codes, width), F32),
        ),
        scratch_shapes=[
            pltpu.VMEM((rows + 2 * PAD, width), F32),
            pltpu.VMEM((rows + 2 * PAD, ROWS), F32),
            pltpu.VMEM((rows, width), F32),
        ],
        compiler_params=params(24),
        name="hidden_grads",
    )(*operands, *tokens)


def gen_blocks_kernel(order, gen_ref, token_ref, out_ref):
    columns = gen_ref.shape[0]
    members, _, width = out_ref.shape
    out_ref[...] = jnp.zeros_like(out_ref)
    for k in range(members):
        at = pl.multiple_of(order[k] * width, width)
        out_ref[k, 0:columns] = gen_ref[:, pl.ds(at, width)]


def gen_blocks(order, gen_rows, width, token):
    columns, depth = gen_rows.shape
    members = depth // width
    return pl.pallas_call(
        gen_blocks_kernel,
        grid_spec=pltpu.PrefetchScalarGridSpec(
            num_scalar_prefetch=1,
            grid=(1,),
            in_specs=[
                pl.BlockSpec((columns, depth), lambda i, o: (0, 0)),
                pl.BlockSpec(memory_space=pltpu.HBM),
            ],
            out_specs=pl.BlockSpec((members, ROWS, width), lambda i, o: (0, 0, 0)),
        ),
        out_shape=jax.ShapeDtypeStruct((members, ROWS, width), BF16),
        compiler_params=params(24),
        name="gen_blocks",
    )(order, gen_rows, token)


def gen_grads_kernel(logit_ref, hidden_ref, out_ref):
    width = hidden_ref.shape[2]
    for piece in range(hidden_ref.shape[0]):
        out_ref[:, piece * width : (piece + 1) * width] = jnp.dot(
            logit_ref[...], hidden_ref[piece], preferred_element_type=F32
        )


def gen_grads(logit_grad, hidden_full):
    members, rows, width = hidden_full.shape
    heads = logit_grad.shape[0]
    return pl.pallas_call(
        gen_grads_kernel,
        out_shape=jax.ShapeDtypeStruct((heads, members * width), F32),
        compiler_params=params(24),
        name="gen_grads",
    )(logit_grad, hidden_full)


def add_up(values):
    total = values[0].astype(F32)
    for value in values[1:]:
        total = total + value.astype(F32)
    return total


def swap_pairs(pairs):
    return [pairs[0]] + [flip(pairs[z], "tp", z) for z in (1, 2, 3)]


def body(
    embeddings,
    span_mask,
    sentinel_id,
    sentinel_table,
    gen_weight,
    up_weight,
    down_weight,
    cotangent,
):
    rows, width = embeddings.shape
    codes = sentinel_table.shape[0]
    members = lax.axis_size("tp")
    me = lax.axis_index("tp")
    order = jnp.arange(members, dtype=jnp.int32) ^ me.astype(jnp.int32)

    sentinel_codes = jnp.arange(codes, dtype=jnp.int32)
    onehot = (sentinel_id[:, None] == sentinel_codes[None, :]).astype(BF16)
    picked = jnp.dot(onehot, sentinel_table, preferred_element_type=F32).astype(BF16)
    hidden = jnp.where(span_mask[:, None] == 1, picked, embeddings)
    pieces = gather_pieces(hidden)
    cot_full = lax.all_gather(cotangent, "tp", axis=0, tiled=False)

    hidden_full, edges, flat, taps = hidden_logits(order, pieces, gen_weight.T)
    high_full, low_full = edges[0], edges[1]
    count = lax.axis_size("seq")
    low_full = lax.ppermute(low_full, "seq", [(i, i + 1) for i in range(count - 1)])
    high_full = lax.ppermute(high_full, "seq", [(i + 1, i) for i in range(count - 1)])
    middle_grad = grad_middle(cot_full, down_weight)
    flat_full = gather_small(flat, (middle_grad,))

    columns = gen_weight.shape[1]
    gen_full = gen_blocks(order, gen_weight.T, width, hidden_full)
    gen_full = exchange(gen_full, (1, 2))

    summed, act, middle, *back_own = layer(
        order,
        hidden_full,
        low_full,
        high_full,
        flat_full,
        up_weight,
        middle_grad,
        cot_full,
        (gen_full,),
    )
    back_pairs = swap_pairs(back_own)
    summed = lax.psum_scatter(summed, "seq", scatter_dimension=0, tiled=False)
    tap_low, tap_high = halo(taps)
    out_own = spread(order, middle, down_weight, (tap_low,))
    out_pairs = swap_pairs(out_own)
    gen_full = exchange(gen_full, (4,)).reshape(members * ROWS, width)

    out_last = flip(add_up([pair[1] for pair in out_pairs]).astype(BF16), "tp", 4)
    back_last = flip(add_up([pair[1] for pair in back_pairs]).astype(BF16), "tp", 4)
    low = lax.dynamic_index_in_dim(low_full, me, 0, keepdims=False)
    high = lax.dynamic_index_in_dim(high_full, me, 0, keepdims=False)
    grad, logit_grad = kernel_grads(
        back_pairs,
        back_last,
        cotangent,
        hidden,
        low,
        high,
        taps,
        (gen_full, tap_low, tap_high, out_own[0]),
    )
    grad_low, grad_high = halo(grad.astype(BF16))
    logit_full = gather_small(logit_grad).reshape(members * ROWS, rows)
    gen_sum = sum_over_seq(gen_grads(logit_grad, hidden_full), (1,))
    embed_grad, table_part = hidden_grads(
        (
            grad,
            grad_low,
            grad_high,
            taps,
            tap_low,
            tap_high,
            logit_full,
            gen_full,
            span_mask[:, None],
            sentinel_id[None, :],
        ),
        codes,
        (gen_sum, out_last),
    )
    gen_sum = sum_over_seq(gen_sum, (8, 2, 4))
    gen_grad = gen_sum[:columns].T
    table_grad = sum_over_seq(table_part)

    total = add_up([pair[0] for pair in out_pairs] + [out_last])
    layer_output = (act.astype(F32) + total).astype(BF16)

    chunk = summed.shape[0] // 2
    up_grad = summed[:chunk].astype(F32)
    down_grad = summed[chunk:].astype(F32).T
    return (layer_output, embed_grad, table_grad, gen_grad, up_grad, down_grad)


def solution(mesh):
    placed = (
        P("seq", "tp"),
        P("seq"),
        P("seq"),
        P(None, "tp"),
        P(None, "tp"),
        P(None, "tp"),
        P("tp", None),
        P("seq", "tp"),
    )
    return jax.shard_map(
        body,
        mesh=mesh,
        in_specs=placed,
        out_specs=(
            P("seq", "tp"),
            P("seq", "tp"),
            P(None, "tp"),
            P(None, "tp"),
            P("seq", "tp"),
            P("tp", "seq"),
        ),
        check_vma=False,
    )
```

```python
import functools

import jax
import jax.numpy as jnp
from jax import lax
from jax.experimental import pallas as pl
from jax.experimental.pallas import tpu as pltpu
from jax.sharding import PartitionSpec as P

KW = 15
REACH = 7
PAD = 8
ROWS = 32
F32 = jnp.float32
BF16 = jnp.bfloat16
NT = (((1,), (1,)), ((), ()))
TN = (((0,), (0,)), ((), ()))


def params(megabytes=60):
    return pltpu.CompilerParams(vmem_limit_bytes=megabytes << 20)


def after(value, *others):
    return lax.optimization_barrier((value, *others))[0]


def ordered(kernel, inputs, tokens):
    def run(*refs):
        kernel(*refs[:inputs], *refs[inputs + len(tokens) :])

    return run, [pl.BlockSpec(memory_space=pltpu.HBM) for _ in tokens]


def flip(value, axis, bit):
    count = lax.axis_size(axis)
    return lax.ppermute(value, axis, [(i, i ^ bit) for i in range(count)])


def halo(value):
    count = lax.axis_size("seq")
    forward = [(i, i + 1) for i in range(count - 1)]
    backward = [(i + 1, i) for i in range(count - 1)]
    low = lax.ppermute(value[-PAD:], "seq", forward)
    high = lax.ppermute(value[:PAD], "seq", backward)
    return low, high


def exchange(blocks, bits=(4, 2, 1)):
    shape = blocks.shape
    cube = blocks.reshape((2, 2, 2) + shape[1:])
    for bit in bits:
        place = {4: 0, 2: 1, 1: 2}[bit]
        keep = lax.index_in_dim(cube, 0, place, keepdims=True)
        send = lax.index_in_dim(cube, 1, place, keepdims=True)
        cube = jnp.concatenate([keep, flip(send, "tp", bit)], axis=place)
    return cube.reshape(shape)


def gather_small(value, beside=()):
    blocks = value[None]
    for bit in (1, 2, 4):
        other = flip(blocks, "tp", bit)
        if bit == 4 and beside:
            other = after(other, *beside)
        blocks = jnp.concatenate([blocks, other], axis=0)
    return blocks


def gather_far_first(value):
    blocks = value[None]
    for bit in (4, 2, 1):
        both = jnp.stack([blocks, flip(blocks, "tp", bit)], axis=1)
        blocks = both.reshape((-1,) + value.shape)
    return blocks


def sum_over_seq(value, bits=(1, 8, 2, 4)):
    for bit in bits:
        sent = value.astype(BF16)
        value = sent.astype(F32) + flip(sent, "seq", bit).astype(F32)
    return value


def gather_pieces(value):
    half = value.shape[0] // 2
    four = flip(value, "tp", 4)
    one = flip(value, "tp", 1)
    three = flip(value, "tp", 3)
    five = flip(four, "tp", 1)
    seven = flip(four, "tp", 3)
    two_a = flip(one[:half], "tp", 3)
    two_b = flip(three[half:], "tp", 1)
    six_a = flip(five[:half], "tp", 3)
    six_b = flip(seven[half:], "tp", 1)
    return value, one, three, four, five, seven, two_a, two_b, six_a, six_b


def hidden_logits_kernel(order, *refs):
    pieces = refs[:10]
    gen_ref, out_ref, edge_ref, flat_ref, tap_ref, full_ref, sems = refs[10:]
    members, rows, width = full_ref.shape
    half = rows // 2
    targets = [full_ref.at[order[at]] for at in (0, 1, 3, 4, 5, 7)]
    for at in (2, 6):
        targets.append(full_ref.at[order[at], 0:half])
        targets.append(full_ref.at[order[at], half:rows])
    copies = [
        pltpu.make_async_copy(ref, target, sems.at[index])
        for index, (ref, target) in enumerate(zip(pieces, targets))
    ]
    for copy in copies:
        copy.start()
    for copy in copies:
        copy.wait()
    backs = [
        pltpu.make_async_copy(full_ref.at[piece], out_ref.at[piece], sems.at[len(pieces) + piece])
        for piece in range(members)
    ]
    for copy in backs:
        copy.start()
    logits = jnp.zeros((gen_ref.shape[0], rows), F32)
    for piece in range(members):
        edge_ref[0, piece] = full_ref[piece, 0:PAD]
        edge_ref[1, piece] = full_ref[piece, rows - PAD :]
        logits = logits + lax.dot_general(
            gen_ref[:, piece * width : (piece + 1) * width],
            full_ref[piece],
            NT,
            preferred_element_type=F32,
        )
    exps = jnp.exp(logits)
    first = exps[0:KW]
    second = exps[KW : 2 * KW]
    first = first / jnp.sum(first, axis=0, keepdims=True)
    second = second / jnp.sum(second, axis=0, keepdims=True)
    blank = jnp.zeros((ROWS - 2 * KW, rows), F32)
    flat = jnp.concatenate([first, second, blank], axis=0)
    flat_ref[...] = flat
    tap_ref[...] = flat.T
    for copy in backs:
        copy.wait()


def hidden_logits(order, pieces, gen_rows):
    rows, width = pieces[0].shape
    columns, depth = gen_rows.shape
    members = depth // width
    whole = [pl.BlockSpec(memory_space=pltpu.HBM) for _ in pieces]
    return pl.pallas_call(
        hidden_logits_kernel,
        grid_spec=pltpu.PrefetchScalarGridSpec(
            num_scalar_prefetch=1,
            grid=(1,),
            in_specs=whole + [pl.BlockSpec((columns, depth), lambda i, o: (0, 0))],
            out_specs=[
                pl.BlockSpec(memory_space=pltpu.HBM),
                pl.BlockSpec((2, members, PAD, width), lambda i, o: (0, 0, 0, 0)),
                pl.BlockSpec((ROWS, rows), lambda i, o: (0, 0)),
                pl.BlockSpec((rows, ROWS), lambda i, o: (0, 0)),
            ],
            scratch_shapes=[
                pltpu.VMEM((members, rows, width), BF16),
                pltpu.SemaphoreType.DMA((len(pieces) + members,)),
            ],
        ),
        out_shape=(
            jax.ShapeDtypeStruct((members, rows, width), BF16),
            jax.ShapeDtypeStruct((2, members, PAD, width), BF16),
            jax.ShapeDtypeStruct((ROWS, rows), F32),
            jax.ShapeDtypeStruct((rows, ROWS), F32),
        ),
        compiler_params=params(),
        name="hidden_logits",
    )(order, *pieces, gen_rows)


def layer_kernel(
    order,
    hidden_ref,
    low_ref,
    high_ref,
    flat_one_ref,
    flat_two_ref,
    up_ref,
    grad_ref,
    cot_ref,
    summed_ref,
    own_ref,
    middle_ref,
    zero_ref,
    one_ref,
    two_ref,
    three_ref,
    padded,
    pre,
    pre_grad,
    act,
    up_kept,
    held,
    sems,
):
    index = pl.program_id(0)
    count, rows, width = hidden_ref.shape
    firsts = act.shape[0] // count

    @pl.when(index < firsts)
    def _():
        step = 64
        reach = 2 * step
        heads = 2
        head_width = width // heads
        lane = lax.broadcasted_iota(jnp.int32, (step, reach), 1)
        depth = up_ref.shape[0]
        up_kept[pl.ds(pl.multiple_of(index * depth, depth), depth)] = up_ref[...]
        term = None
        for piece, flat_ref in enumerate((flat_one_ref, flat_two_ref)):
            at = count * index + piece
            padded[piece, 0:PAD] = low_ref[piece]
            padded[piece, PAD : PAD + rows] = hidden_ref[piece]
            padded[piece, PAD + rows : 2 * PAD + rows] = high_ref[piece]
            padded[piece, 2 * PAD + rows :] = jnp.zeros((step - 2 * PAD, width), BF16)
            flat = flat_ref[0]
            taps = jnp.concatenate([flat, jnp.zeros((reach - ROWS, rows), F32)], axis=0).T
            for base in range(0, rows, step):
                for head in range(heads):
                    lanes = slice(head * head_width, (head + 1) * head_width)
                    mine = (lane >= head * KW) & (lane < (head + 1) * KW)
                    own = jnp.where(mine, taps[base : base + step], 0.0)
                    own = pltpu.roll(own, (1 - head * KW) % reach, 1)
                    band = pltpu.roll(own, 0, 1, stride=1, stride_axis=0)
                    upper = band.astype(BF16)
                    lower = (band - upper.astype(F32)).astype(BF16)
                    window = padded[piece, base : base + reach, lanes]
                    both = jnp.dot(
                        jnp.concatenate([upper, lower], axis=0),
                        window,
                        preferred_element_type=F32,
                    )
                    value = hidden_ref[piece, base : base + step, lanes].astype(F32)
                    value = value + (both[:step] + both[step:])
                    act[at, base : base + step, lanes] = value.astype(BF16)
            part = jnp.dot(
                act[at],
                up_ref[piece * width : (piece + 1) * width, :],
                preferred_element_type=F32,
            )
            term = part if term is None else term + part

        @pl.when(index == 0)
        def _():
            pre[...] = term

        @pl.when(index > 0)
        def _():
            pre[...] += term

    @pl.when(index == firsts - 1)
    def _():
        scale = 0.7978845608028654
        chunk = 64

        def run(turn, carry):
            at = pl.ds(pl.multiple_of(turn * chunk, chunk), chunk)
            value = pre[at, :]
            square = value * value
            bent = jnp.tanh(scale * (value + 0.044715 * (square * value)))
            middle_ref[at, :] = (0.5 * value * (1.0 + bent)).astype(BF16)
            slope = 0.5 * (1.0 + bent) + 0.5 * value * (1.0 - bent * bent) * (
                scale * (1.0 + 3.0 * 0.044715 * square)
            )
            pre_grad[at, :] = (grad_ref[at, :] * slope).astype(BF16)
            return carry

        lax.fori_loop(0, rows // chunk, run, 0)
        own_ref[...] = act[order[0]]

    turn = index - firsts
    last = act.shape[0] - 1
    per = held.shape[1]
    half = held.shape[2] // 2

    def copies(at, slot):
        return [
            pltpu.make_async_copy(
                held.at[slot, chunk, part * half : (part + 1) * half],
                summed_ref.at[per * at + chunk, part * half : (part + 1) * half],
                sems.at[slot, 2 * chunk + part],
            )
            for chunk in range(per)
            for part in range(2)
        ]

    @pl.when(turn >= 0)
    def _():
        slot = lax.rem(turn, 2)
        up = lax.dot_general(act[turn], pre_grad[...], TN, preferred_element_type=F32)
        down = lax.dot_general(cot_ref[0], middle_ref[...], TN, preferred_element_type=F32)

        @pl.when(turn >= 2)
        def _():
            for copy in copies(turn - 2, slot):
                copy.wait()

        for chunk in range(per):
            lines = slice(chunk * half, (chunk + 1) * half)
            held[slot, chunk, 0:half] = up[lines].astype(BF16)
            held[slot, chunk, half:] = down[lines].astype(BF16)
        for copy in copies(turn, slot):
            copy.start()
        at = pl.multiple_of(order[turn] * width, width)
        result = lax.dot_general(
            pre_grad[...], up_kept[pl.ds(at, width)], NT, preferred_element_type=F32
        ).astype(BF16)
        for z, ref in enumerate((zero_ref, one_ref, two_ref, three_ref)):

            @pl.when(lax.rem(turn, 4) == z)
            def _(ref=ref):
                ref[0] = result

        @pl.when(turn == last)
        def _():
            for copy in copies(turn - 1, 1 - slot):
                copy.wait()
            for copy in copies(turn, slot):
                copy.wait()


def layer(order, hidden_full, low, high, flat_full, up_weight, middle_grad, cot_full, tokens):
    members, rows, width = hidden_full.shape
    units = up_weight.shape[1]
    firsts = members // 2
    chunks = lax.axis_size("seq")
    per = chunks // members
    chunk = width // per
    kernel, token_specs = ordered(layer_kernel, 9, tokens)

    def pair(i):
        return jnp.minimum(i, firsts - 1)

    def turn(i):
        return jnp.maximum(i - firsts, 0)

    return pl.pallas_call(
        kernel,
        grid_spec=pltpu.PrefetchScalarGridSpec(
            num_scalar_prefetch=1,
            grid=(firsts + members,),
            in_specs=[
                pl.BlockSpec((2, rows, width), lambda i, o: (pair(i), 0, 0)),
                pl.BlockSpec((2, PAD, width), lambda i, o: (pair(i), 0, 0)),
                pl.BlockSpec((2, PAD, width), lambda i, o: (pair(i), 0, 0)),
                pl.BlockSpec((1, ROWS, rows), lambda i, o: (o[2 * pair(i)], 0, 0)),
                pl.BlockSpec((1, ROWS, rows), lambda i, o: (o[2 * pair(i) + 1], 0, 0)),
                pl.BlockSpec((2 * width, units), lambda i, o: (pair(i), 0)),
                pl.BlockSpec((rows, units), lambda i, o: (0, 0)),
                pl.BlockSpec((1, rows, width), lambda i, o: (turn(i), 0, 0)),
            ]
            + token_specs,
            out_specs=[
                pl.BlockSpec(memory_space=pltpu.HBM),
                pl.BlockSpec((rows, width), lambda i, o: (0, 0)),
                pl.BlockSpec((rows, units), lambda i, o: (0, 0)),
            ]
            + [pl.BlockSpec((1, rows, width), lambda i, o: (turn(i) // 4, 0, 0))] * 4,
            scratch_shapes=[
                pltpu.VMEM((2, rows + 64, width), BF16),
                pltpu.VMEM((rows, units), F32),
                pltpu.VMEM((rows, units), BF16),
                pltpu.VMEM((members, rows, width), BF16),
                pltpu.VMEM((members * width, units), BF16),
                pltpu.VMEM((2, per, 2 * chunk, units), BF16),
                pltpu.SemaphoreType.DMA((2, 2 * per)),
            ],
        ),
        out_shape=[
            jax.ShapeDtypeStruct((chunks, 2 * chunk, units), BF16),
            jax.ShapeDtypeStruct((rows, width), BF16),
            jax.ShapeDtypeStruct((rows, units), BF16),
        ]
        + [jax.ShapeDtypeStruct((2, rows, width), BF16)] * 4,
        compiler_params=params(),
        name="layer",
    )(
        order,
        hidden_full,
        low,
        high,
        flat_full,
        flat_full,
        up_weight,
        middle_grad,
        cot_full,
        *tokens,
    )


def grad_middle_kernel(cot_ref, *refs):
    out_ref = refs[-1]
    width = cot_ref.shape[2]
    total = jnp.zeros(out_ref.shape, F32)
    for piece in range(cot_ref.shape[0]):
        ref = refs[piece // 2]
        lanes = slice(piece % 2 * width, (piece % 2 + 1) * width)
        total = total + lax.dot_general(
            cot_ref[piece], ref[:, lanes], NT, preferred_element_type=F32
        )
    out_ref[...] = total


def grad_middle(cot_full, down_weight):
    pieces, rows, width = cot_full.shape
    units = down_weight.shape[0]
    block = 256
    parts = pieces // 2
    return pl.pallas_call(
        grad_middle_kernel,
        grid=(units // block,),
        in_specs=[pl.BlockSpec((pieces, rows, width), lambda i: (0, 0, 0))]
        + [pl.BlockSpec((block, 2 * width), lambda i, q=q: (i, q)) for q in range(parts)],
        out_specs=pl.BlockSpec((rows, block), lambda i: (0, i)),
        out_shape=jax.ShapeDtypeStruct((rows, units), F32),
        compiler_params=params(),
        name="grad_middle",
    )(cot_full, *[down_weight] * parts)


def spread_kernel(order, value_ref, weight_ref, *out_refs):
    result = jnp.dot(value_ref[...], weight_ref[...], preferred_element_type=F32).astype(BF16)
    for index, ref in enumerate(out_refs):

        @pl.when(lax.rem(pl.program_id(0), 4) == index)
        def _(ref=ref):
            ref[0] = result


def spread(order, value, weight, tokens):
    rows, units = value.shape
    width = weight.shape[1] // 8
    kernel, token_specs = ordered(spread_kernel, 3, tokens)
    return pl.pallas_call(
        kernel,
        grid_spec=pltpu.PrefetchScalarGridSpec(
            num_scalar_prefetch=1,
            grid=(8,),
            in_specs=[
                pl.BlockSpec((rows, units), lambda k, o: (0, 0)),
                pl.BlockSpec((units, width), lambda k, o: (0, o[k])),
            ]
            + token_specs,
            out_specs=[pl.BlockSpec((1, rows, width), lambda k, o: (k // 4, 0, 0))] * 4,
        ),
        out_shape=[jax.ShapeDtypeStruct((2, rows, width), BF16)] * 4,
        compiler_params=params(),
        name="ffn_out",
    )(order, value, weight, *tokens)


def kernel_grad_kernel(*refs):
    terms = refs[:5]
    cot_ref, hidden_ref, low_ref, high_ref, tap_ref = refs[5:10]
    grad_ref, logit_ref, padded, found_ref = refs[10:]
    rows, width = hidden_ref.shape
    heads = 2
    head_width = width // heads
    padded[0:PAD] = low_ref[...].astype(F32)
    padded[PAD : PAD + rows] = hidden_ref[...].astype(F32)
    padded[PAD + rows :] = high_ref[...].astype(F32)
    step = 32
    lane = lax.broadcasted_iota(jnp.int32, (step, ROWS), 1)

    def run(index, carry):
        base = pl.multiple_of(index * step, step)
        at = pl.ds(base, step)
        grad = terms[0][at, :].astype(F32)
        for ref in terms[1:]:
            grad = grad + ref[at, :].astype(F32)
        grad = grad + cot_ref[at, :].astype(F32)
        grad_ref[at, :] = grad
        taps = tap_ref[at, :]
        found = jnp.zeros((step, ROWS), F32)
        for head in range(heads):
            lanes = slice(head * head_width, (head + 1) * head_width)
            window = padded[pl.ds(base, step + 2 * PAD), lanes]
            part = grad[:, lanes]
            for tap in range(KW):
                column = head * KW + tap
                value = jnp.sum(part * window[tap + 1 : tap + 1 + step], axis=1, keepdims=True)
                found = jnp.where(lane == column, value, found)
        product = taps * found
        in_first = lane < KW
        one = jnp.sum(jnp.where(in_first, product, 0.0), axis=1, keepdims=True)
        two = jnp.sum(jnp.where(in_first, 0.0, product), axis=1, keepdims=True)
        found_ref[at, :] = taps * (found - jnp.where(in_first, one, two))
        return carry

    lax.fori_loop(0, rows // step, run, 0)
    logit_ref[...] = found_ref[...].T.astype(BF16)


def kernel_grads(pairs, last, cotangent, hidden, low, high, taps, tokens):
    rows, width = hidden.shape
    flat = pl.BlockSpec((rows, width), lambda i: (0, 0))
    edge = pl.BlockSpec((PAD, width), lambda i: (0, 0))
    kernel, token_specs = ordered(kernel_grad_kernel, 10, tokens)
    return pl.pallas_call(
        kernel,
        grid=(1,),
        in_specs=[pl.BlockSpec((None, rows, width), lambda i: (0, 0, 0))] * 4
        + [flat, flat, flat, edge, edge, pl.BlockSpec((rows, ROWS), lambda i: (0, 0))]
        + token_specs,
        out_specs=[flat, pl.BlockSpec((ROWS, rows), lambda i: (0, 0))],
        out_shape=(
            jax.ShapeDtypeStruct((rows, width), F32),
            jax.ShapeDtypeStruct((ROWS, rows), BF16),
        ),
        scratch_shapes=[
            pltpu.VMEM((rows + 2 * PAD, width), F32),
            pltpu.VMEM((rows, ROWS), F32),
        ],
        compiler_params=params(24),
        name="kernel_grads",
    )(*pairs, last, cotangent, hidden, low, high, taps, *tokens)


def hidden_grad_kernel(
    grad_ref,
    glow_ref,
    ghigh_ref,
    tap_ref,
    tlow_ref,
    thigh_ref,
    logit_ref,
    gen_ref,
    mask_ref,
    code_ref,
    embed_ref,
    table_ref,
    padded,
    tapped,
    back,
):
    rows, width = grad_ref.shape
    heads = 2
    head_width = width // heads
    padded[0:PAD] = glow_ref[...].astype(F32)
    padded[PAD : PAD + rows] = grad_ref[...]
    padded[PAD + rows :] = ghigh_ref[...].astype(F32)
    tapped[0:PAD] = tlow_ref[...]
    tapped[PAD : PAD + rows] = tap_ref[...]
    tapped[PAD + rows :] = thigh_ref[...]
    back[...] = lax.dot_general(logit_ref[...], gen_ref[...], TN, preferred_element_type=F32)
    step = 32

    def run(index, carry):
        base = pl.multiple_of(index * step, step)
        at = pl.ds(base, step)
        picked = mask_ref[at, :] == 1
        taps = tapped[pl.ds(base, step + 2 * PAD), :]
        for head in range(heads):
            lanes = slice(head * head_width, (head + 1) * head_width)
            window = padded[pl.ds(base, step + 2 * PAD), lanes]
            total = window[PAD : PAD + step] + back[at, lanes]
            for tap in range(KW):
                column = head * KW + tap
                lower = 2 * PAD - 1 - tap
                total = (
                    total
                    + taps[lower : lower + step, column : column + 1]
                    * window[lower : lower + step]
                )
            embed_ref[at, lanes] = jnp.where(picked, 0.0, total)
            back[at, lanes] = jnp.where(picked, total, 0.0)
        return carry

    lax.fori_loop(0, rows // step, run, 0)
    codes = lax.broadcasted_iota(jnp.int32, (table_ref.shape[0], rows), 0)
    chosen = jnp.where(codes == code_ref[...], 1.0, 0.0).astype(BF16)
    value = back[...]
    upper = value.astype(BF16)
    lower = (value - upper.astype(F32)).astype(BF16)
    table_ref[...] = jnp.dot(chosen, upper, preferred_element_type=F32) + jnp.dot(
        chosen, lower, preferred_element_type=F32
    )


def hidden_grads(operands, codes, tokens):
    rows, width = operands[0].shape
    kernel, token_specs = ordered(hidden_grad_kernel, len(operands), tokens)
    whole = [pl.BlockSpec(o.shape, lambda i: (0, 0)) for o in operands]
    return pl.pallas_call(
        kernel,
        grid=(1,),
        in_specs=whole + token_specs,
        out_specs=[
            pl.BlockSpec((rows, width), lambda i: (0, 0)),
            pl.BlockSpec((codes, width), lambda i: (0, 0)),
        ],
        out_shape=(
            jax.ShapeDtypeStruct((rows, width), F32),
            jax.ShapeDtypeStruct((codes, width), F32),
        ),
        scratch_shapes=[
            pltpu.VMEM((rows + 2 * PAD, width), F32),
            pltpu.VMEM((rows + 2 * PAD, ROWS), F32),
            pltpu.VMEM((rows, width), F32),
        ],
        compiler_params=params(24),
        name="hidden_grads",
    )(*operands, *tokens)


def gen_blocks_kernel(order, gen_ref, token_ref, out_ref):
    columns = gen_ref.shape[0]
    members, _, width = out_ref.shape
    out_ref[...] = jnp.zeros_like(out_ref)
    for k in range(members):
        at = pl.multiple_of(order[k] * width, width)
        out_ref[k, 0:columns] = gen_ref[:, pl.ds(at, width)]


def gen_blocks(order, gen_rows, width, token):
    columns, depth = gen_rows.shape
    members = depth // width
    return pl.pallas_call(
        gen_blocks_kernel,
        grid_spec=pltpu.PrefetchScalarGridSpec(
            num_scalar_prefetch=1,
            grid=(1,),
            in_specs=[
                pl.BlockSpec((columns, depth), lambda i, o: (0, 0)),
                pl.BlockSpec(memory_space=pltpu.HBM),
            ],
            out_specs=pl.BlockSpec((members, ROWS, width), lambda i, o: (0, 0, 0)),
        ),
        out_shape=jax.ShapeDtypeStruct((members, ROWS, width), BF16),
        compiler_params=params(24),
        name="gen_blocks",
    )(order, gen_rows, token)


def gen_grads_kernel(logit_ref, hidden_ref, out_ref):
    width = hidden_ref.shape[2]
    for piece in range(hidden_ref.shape[0]):
        out_ref[:, piece * width : (piece + 1) * width] = jnp.dot(
            logit_ref[...], hidden_ref[piece], preferred_element_type=F32
        )


def gen_grads(logit_grad, hidden_full):
    members, rows, width = hidden_full.shape
    heads = logit_grad.shape[0]
    return pl.pallas_call(
        gen_grads_kernel,
        out_shape=jax.ShapeDtypeStruct((heads, members * width), F32),
        compiler_params=params(24),
        name="gen_grads",
    )(logit_grad, hidden_full)


def add_up(values):
    total = values[0].astype(F32)
    for value in values[1:]:
        total = total + value.astype(F32)
    return total


def swap_pairs(pairs):
    return [pairs[0]] + [flip(pairs[z], "tp", z) for z in (1, 2, 3)]


def body(
    embeddings,
    span_mask,
    sentinel_id,
    sentinel_table,
    gen_weight,
    up_weight,
    down_weight,
    cotangent,
):
    rows, width = embeddings.shape
    codes = sentinel_table.shape[0]
    members = lax.axis_size("tp")
    me = lax.axis_index("tp")
    order = jnp.arange(members, dtype=jnp.int32) ^ me.astype(jnp.int32)

    sentinel_codes = jnp.arange(codes, dtype=jnp.int32)
    onehot = (sentinel_id[:, None] == sentinel_codes[None, :]).astype(BF16)
    picked = jnp.dot(onehot, sentinel_table, preferred_element_type=F32).astype(BF16)
    hidden = jnp.where(span_mask[:, None] == 1, picked, embeddings)
    pieces = gather_pieces(hidden)
    cot_full = lax.all_gather(cotangent, "tp", axis=0, tiled=False)

    hidden_full, edges, flat, taps = hidden_logits(order, pieces, gen_weight.T)
    high_full, low_full = edges[0], edges[1]
    count = lax.axis_size("seq")
    low_full = lax.ppermute(low_full, "seq", [(i, i + 1) for i in range(count - 1)])
    high_full = lax.ppermute(high_full, "seq", [(i + 1, i) for i in range(count - 1)])
    middle_grad = grad_middle(cot_full, down_weight)
    flat_full = gather_small(flat, (middle_grad,))

    columns = gen_weight.shape[1]
    gen_full = gen_blocks(order, gen_weight.T, width, hidden_full)
    gen_full = exchange(gen_full, (1, 2))

    summed, act, middle, *back_own = layer(
        order,
        hidden_full,
        low_full,
        high_full,
        flat_full,
        up_weight,
        middle_grad,
        cot_full,
        (gen_full,),
    )
    back_pairs = swap_pairs(back_own)
    summed = lax.psum_scatter(summed, "seq", scatter_dimension=0, tiled=False)
    gen_full = exchange(gen_full, (4,))
    tap_low, tap_high = halo(taps)
    out_own = spread(order, middle, down_weight, (gen_full, tap_low, tap_high))
    out_pairs = swap_pairs(out_own)
    gen_full = gen_full.reshape(members * ROWS, width)

    out_last = flip(add_up([pair[1] for pair in out_pairs]).astype(BF16), "tp", 4)
    back_last = flip(add_up([pair[1] for pair in back_pairs]).astype(BF16), "tp", 4)
    low = lax.dynamic_index_in_dim(low_full, me, 0, keepdims=False)
    high = lax.dynamic_index_in_dim(high_full, me, 0, keepdims=False)
    grad, logit_grad = kernel_grads(
        back_pairs,
        back_last,
        cotangent,
        hidden,
        low,
        high,
        taps,
        (gen_full, tap_low, tap_high, out_own[0]),
    )
    grad_low, grad_high = halo(grad.astype(BF16))
    logit_full = gather_far_first(logit_grad).reshape(members * ROWS, rows)
    gen_sum = sum_over_seq(gen_grads(logit_grad, hidden_full), (1,))
    embed_grad, table_part = hidden_grads(
        (
            grad,
            grad_low,
            grad_high,
            taps,
            tap_low,
            tap_high,
            logit_full,
            gen_full,
            span_mask[:, None],
            sentinel_id[None, :],
        ),
        codes,
        (gen_sum, out_last),
    )
    gen_sum = sum_over_seq(gen_sum, (8, 2, 4))
    gen_grad = gen_sum[:columns].T
    table_grad = sum_over_seq(table_part)

    total = add_up([pair[0] for pair in out_pairs] + [out_last])
    layer_output = (act.astype(F32) + total).astype(BF16)

    chunk = summed.shape[0] // 2
    up_grad = summed[:chunk].astype(F32)
    down_grad = summed[chunk:].astype(F32).T
    return (layer_output, embed_grad, table_grad, gen_grad, up_grad, down_grad)


def solution(mesh):
    placed = (
        P("seq", "tp"),
        P("seq"),
        P("seq"),
        P(None, "tp"),
        P(None, "tp"),
        P(None, "tp"),
        P("tp", None),
        P("seq", "tp"),
    )
    return jax.shard_map(
        body,
        mesh=mesh,
        in_specs=placed,
        out_specs=(
            P("seq", "tp"),
            P("seq", "tp"),
            P(None, "tp"),
            P(None, "tp"),
            P("seq", "tp"),
            P("tp", "seq"),
        ),
        check_vma=False,
    )
```

```python
import functools

import jax
import jax.numpy as jnp
from jax import lax
from jax.experimental import pallas as pl
from jax.experimental.pallas import tpu as pltpu
from jax.sharding import PartitionSpec as P

KW = 15
REACH = 7
PAD = 8
ROWS = 32
F32 = jnp.float32
BF16 = jnp.bfloat16
NT = (((1,), (1,)), ((), ()))
TN = (((0,), (0,)), ((), ()))


def params(megabytes=60):
    return pltpu.CompilerParams(vmem_limit_bytes=megabytes << 20)


def after(value, *others):
    return lax.optimization_barrier((value, *others))[0]


def ordered(kernel, inputs, tokens):
    def run(*refs):
        kernel(*refs[:inputs], *refs[inputs + len(tokens) :])

    return run, [pl.BlockSpec(memory_space=pltpu.HBM) for _ in tokens]


def flip(value, axis, bit):
    count = lax.axis_size(axis)
    return lax.ppermute(value, axis, [(i, i ^ bit) for i in range(count)])


def halo(value):
    count = lax.axis_size("seq")
    forward = [(i, i + 1) for i in range(count - 1)]
    backward = [(i + 1, i) for i in range(count - 1)]
    low = lax.ppermute(value[-PAD:], "seq", forward)
    high = lax.ppermute(value[:PAD], "seq", backward)
    return low, high


def exchange(blocks, bits=(4, 2, 1)):
    shape = blocks.shape
    cube = blocks.reshape((2, 2, 2) + shape[1:])
    for bit in bits:
        place = {4: 0, 2: 1, 1: 2}[bit]
        keep = lax.index_in_dim(cube, 0, place, keepdims=True)
        send = lax.index_in_dim(cube, 1, place, keepdims=True)
        cube = jnp.concatenate([keep, flip(send, "tp", bit)], axis=place)
    return cube.reshape(shape)


def gather_small(value, beside=()):
    blocks = value[None]
    for bit in (1, 2, 4):
        other = flip(blocks, "tp", bit)
        if bit == 4 and beside:
            other = after(other, *beside)
        blocks = jnp.concatenate([blocks, other], axis=0)
    return blocks


def gather_far_first(value):
    blocks = value[None]
    for bit in (4, 2, 1):
        both = jnp.stack([blocks, flip(blocks, "tp", bit)], axis=1)
        blocks = both.reshape((-1,) + value.shape)
    return blocks


def sum_over_seq(value, bits=(1, 8, 2, 4)):
    for bit in bits:
        sent = value.astype(BF16)
        value = sent.astype(F32) + flip(sent, "seq", bit).astype(F32)
    return value


def gather_pieces(value):
    half = value.shape[0] // 2
    four = flip(value, "tp", 4)
    one = flip(value, "tp", 1)
    three = flip(value, "tp", 3)
    five = flip(four, "tp", 1)
    seven = flip(four, "tp", 3)
    two_a = flip(one[:half], "tp", 3)
    two_b = flip(three[half:], "tp", 1)
    six_a = flip(five[:half], "tp", 3)
    six_b = flip(seven[half:], "tp", 1)
    return value, one, three, four, five, seven, two_a, two_b, six_a, six_b


def hidden_logits_kernel(order, *refs):
    pieces = refs[:10]
    gen_ref, out_ref, edge_ref, flat_ref, tap_ref, full_ref, sems = refs[10:]
    members, rows, width = full_ref.shape
    half = rows // 2
    targets = [full_ref.at[order[at]] for at in (0, 1, 3, 4, 5, 7)]
    for at in (2, 6):
        targets.append(full_ref.at[order[at], 0:half])
        targets.append(full_ref.at[order[at], half:rows])
    copies = [
        pltpu.make_async_copy(ref, target, sems.at[index])
        for index, (ref, target) in enumerate(zip(pieces, targets))
    ]
    for copy in copies:
        copy.start()
    for copy in copies:
        copy.wait()
    backs = [
        pltpu.make_async_copy(full_ref.at[piece], out_ref.at[piece], sems.at[len(pieces) + piece])
        for piece in range(members)
    ]
    for copy in backs:
        copy.start()
    logits = jnp.zeros((gen_ref.shape[0], rows), F32)
    for piece in range(members):
        edge_ref[0, piece] = full_ref[piece, 0:PAD]
        edge_ref[1, piece] = full_ref[piece, rows - PAD :]
        logits = logits + lax.dot_general(
            gen_ref[:, piece * width : (piece + 1) * width],
            full_ref[piece],
            NT,
            preferred_element_type=F32,
        )
    exps = jnp.exp(logits)
    first = exps[0:KW]
    second = exps[KW : 2 * KW]
    first = first / jnp.sum(first, axis=0, keepdims=True)
    second = second / jnp.sum(second, axis=0, keepdims=True)
    blank = jnp.zeros((ROWS - 2 * KW, rows), F32)
    flat = jnp.concatenate([first, second, blank], axis=0)
    flat_ref[...] = flat
    tap_ref[...] = flat.T
    for copy in backs:
        copy.wait()


def hidden_logits(order, pieces, gen_rows):
    rows, width = pieces[0].shape
    columns, depth = gen_rows.shape
    members = depth // width
    whole = [pl.BlockSpec(memory_space=pltpu.HBM) for _ in pieces]
    return pl.pallas_call(
        hidden_logits_kernel,
        grid_spec=pltpu.PrefetchScalarGridSpec(
            num_scalar_prefetch=1,
            grid=(1,),
            in_specs=whole + [pl.BlockSpec((columns, depth), lambda i, o: (0, 0))],
            out_specs=[
                pl.BlockSpec(memory_space=pltpu.HBM),
                pl.BlockSpec((2, members, PAD, width), lambda i, o: (0, 0, 0, 0)),
                pl.BlockSpec((ROWS, rows), lambda i, o: (0, 0)),
                pl.BlockSpec((rows, ROWS), lambda i, o: (0, 0)),
            ],
            scratch_shapes=[
                pltpu.VMEM((members, rows, width), BF16),
                pltpu.SemaphoreType.DMA((len(pieces) + members,)),
            ],
        ),
        out_shape=(
            jax.ShapeDtypeStruct((members, rows, width), BF16),
            jax.ShapeDtypeStruct((2, members, PAD, width), BF16),
            jax.ShapeDtypeStruct((ROWS, rows), F32),
            jax.ShapeDtypeStruct((rows, ROWS), F32),
        ),
        compiler_params=params(),
        name="hidden_logits",
    )(order, *pieces, gen_rows)


def layer_kernel(
    order,
    hidden_ref,
    low_ref,
    high_ref,
    flat_one_ref,
    flat_two_ref,
    up_ref,
    grad_ref,
    cot_ref,
    summed_ref,
    own_ref,
    middle_ref,
    zero_ref,
    one_ref,
    two_ref,
    three_ref,
    padded,
    pre,
    pre_grad,
    act,
    up_kept,
    held,
    sems,
):
    index = pl.program_id(0)
    count, rows, width = hidden_ref.shape
    firsts = act.shape[0] // count

    @pl.when(index < firsts)
    def _():
        step = 64
        reach = 2 * step
        heads = 2
        head_width = width // heads
        lane = lax.broadcasted_iota(jnp.int32, (step, reach), 1)
        depth = up_ref.shape[0]
        up_kept[pl.ds(pl.multiple_of(index * depth, depth), depth)] = up_ref[...]
        term = None
        for piece, flat_ref in enumerate((flat_one_ref, flat_two_ref)):
            at = count * index + piece
            padded[piece, 0:PAD] = low_ref[piece]
            padded[piece, PAD : PAD + rows] = hidden_ref[piece]
            padded[piece, PAD + rows : 2 * PAD + rows] = high_ref[piece]
            padded[piece, 2 * PAD + rows :] = jnp.zeros((step - 2 * PAD, width), BF16)
            flat = flat_ref[0]
            taps = jnp.concatenate([flat, jnp.zeros((reach - ROWS, rows), F32)], axis=0).T
            for base in range(0, rows, step):
                for head in range(heads):
                    lanes = slice(head * head_width, (head + 1) * head_width)
                    mine = (lane >= head * KW) & (lane < (head + 1) * KW)
                    own = jnp.where(mine, taps[base : base + step], 0.0)
                    own = pltpu.roll(own, (1 - head * KW) % reach, 1)
                    band = pltpu.roll(own, 0, 1, stride=1, stride_axis=0)
                    upper = band.astype(BF16)
                    lower = (band - upper.astype(F32)).astype(BF16)
                    window = padded[piece, base : base + reach, lanes]
                    both = jnp.dot(
                        jnp.concatenate([upper, lower], axis=0),
                        window,
                        preferred_element_type=F32,
                    )
                    value = hidden_ref[piece, base : base + step, lanes].astype(F32)
                    value = value + (both[:step] + both[step:])
                    act[at, base : base + step, lanes] = value.astype(BF16)
            part = jnp.dot(
                act[at],
                up_ref[piece * width : (piece + 1) * width, :],
                preferred_element_type=F32,
            )
            term = part if term is None else term + part

        @pl.when(index == 0)
        def _():
            pre[...] = term

        @pl.when(index > 0)
        def _():
            pre[...] += term

    @pl.when(index == firsts - 1)
    def _():
        scale = 0.7978845608028654
        chunk = 64

        def run(turn, carry):
            at = pl.ds(pl.multiple_of(turn * chunk, chunk), chunk)
            value = pre[at, :]
            square = value * value
            bent = jnp.tanh(scale * (value + 0.044715 * (square * value)))
            middle_ref[at, :] = (0.5 * value * (1.0 + bent)).astype(BF16)
            slope = 0.5 * (1.0 + bent) + 0.5 * value * (1.0 - bent * bent) * (
                scale * (1.0 + 3.0 * 0.044715 * square)
            )
            pre_grad[at, :] = (grad_ref[at, :] * slope).astype(BF16)
            return carry

        lax.fori_loop(0, rows // chunk, run, 0)
        own_ref[...] = act[order[0]]

    turn = index - firsts
    last = act.shape[0] - 1
    per = held.shape[1]
    half = held.shape[2] // 2

    def copies(at, slot):
        return [
            pltpu.make_async_copy(
                held.at[slot, chunk, part * half : (part + 1) * half],
                summed_ref.at[per * at + chunk, part * half : (part + 1) * half],
                sems.at[slot, 2 * chunk + part],
            )
            for chunk in range(per)
            for part in range(2)
        ]

    @pl.when(turn >= 0)
    def _():
        slot = lax.rem(turn, 2)
        up = lax.dot_general(act[turn], pre_grad[...], TN, preferred_element_type=F32)
        down = lax.dot_general(cot_ref[0], middle_ref[...], TN, preferred_element_type=F32)

        @pl.when(turn >= 2)
        def _():
            for copy in copies(turn - 2, slot):
                copy.wait()

        for chunk in range(per):
            lines = slice(chunk * half, (chunk + 1) * half)
            held[slot, chunk, 0:half] = up[lines].astype(BF16)
            held[slot, chunk, half:] = down[lines].astype(BF16)
        for copy in copies(turn, slot):
            copy.start()
        at = pl.multiple_of(order[turn] * width, width)
        result = lax.dot_general(
            pre_grad[...], up_kept[pl.ds(at, width)], NT, preferred_element_type=F32
        ).astype(BF16)
        for z, ref in enumerate((zero_ref, one_ref, two_ref, three_ref)):

            @pl.when(lax.rem(turn, 4) == z)
            def _(ref=ref):
                ref[0] = result

        @pl.when(turn == last)
        def _():
            for copy in copies(turn - 1, 1 - slot):
                copy.wait()
            for copy in copies(turn, slot):
                copy.wait()


def layer(order, hidden_full, low, high, flat_full, up_weight, middle_grad, cot_full, tokens):
    members, rows, width = hidden_full.shape
    units = up_weight.shape[1]
    firsts = members // 2
    chunks = lax.axis_size("seq")
    per = chunks // members
    chunk = width // per
    kernel, token_specs = ordered(layer_kernel, 9, tokens)

    def pair(i):
        return jnp.minimum(i, firsts - 1)

    def turn(i):
        return jnp.maximum(i - firsts, 0)

    return pl.pallas_call(
        kernel,
        grid_spec=pltpu.PrefetchScalarGridSpec(
            num_scalar_prefetch=1,
            grid=(firsts + members,),
            in_specs=[
                pl.BlockSpec((2, rows, width), lambda i, o: (pair(i), 0, 0)),
                pl.BlockSpec((2, PAD, width), lambda i, o: (pair(i), 0, 0)),
                pl.BlockSpec((2, PAD, width), lambda i, o: (pair(i), 0, 0)),
                pl.BlockSpec((1, ROWS, rows), lambda i, o: (o[2 * pair(i)], 0, 0)),
                pl.BlockSpec((1, ROWS, rows), lambda i, o: (o[2 * pair(i) + 1], 0, 0)),
                pl.BlockSpec((2 * width, units), lambda i, o: (pair(i), 0)),
                pl.BlockSpec((rows, units), lambda i, o: (0, 0)),
                pl.BlockSpec((1, rows, width), lambda i, o: (turn(i), 0, 0)),
            ]
            + token_specs,
            out_specs=[
                pl.BlockSpec(memory_space=pltpu.HBM),
                pl.BlockSpec((rows, width), lambda i, o: (0, 0)),
                pl.BlockSpec((rows, units), lambda i, o: (0, 0)),
            ]
            + [pl.BlockSpec((1, rows, width), lambda i, o: (turn(i) // 4, 0, 0))] * 4,
            scratch_shapes=[
                pltpu.VMEM((2, rows + 64, width), BF16),
                pltpu.VMEM((rows, units), F32),
                pltpu.VMEM((rows, units), BF16),
                pltpu.VMEM((members, rows, width), BF16),
                pltpu.VMEM((members * width, units), BF16),
                pltpu.VMEM((2, per, 2 * chunk, units), BF16),
                pltpu.SemaphoreType.DMA((2, 2 * per)),
            ],
        ),
        out_shape=[
            jax.ShapeDtypeStruct((chunks, 2 * chunk, units), BF16),
            jax.ShapeDtypeStruct((rows, width), BF16),
            jax.ShapeDtypeStruct((rows, units), BF16),
        ]
        + [jax.ShapeDtypeStruct((2, rows, width), BF16)] * 4,
        compiler_params=params(),
        name="layer",
    )(
        order,
        hidden_full,
        low,
        high,
        flat_full,
        flat_full,
        up_weight,
        middle_grad,
        cot_full,
        *tokens,
    )


def grad_middle_kernel(cot_ref, *refs):
    out_ref = refs[-1]
    width = cot_ref.shape[2]
    total = jnp.zeros(out_ref.shape, F32)
    for piece in range(cot_ref.shape[0]):
        ref = refs[piece // 2]
        lanes = slice(piece % 2 * width, (piece % 2 + 1) * width)
        total = total + lax.dot_general(
            cot_ref[piece], ref[:, lanes], NT, preferred_element_type=F32
        )
    out_ref[...] = total


def grad_middle(cot_full, down_weight):
    pieces, rows, width = cot_full.shape
    units = down_weight.shape[0]
    block = 256
    parts = pieces // 2
    return pl.pallas_call(
        grad_middle_kernel,
        grid=(units // block,),
        in_specs=[pl.BlockSpec((pieces, rows, width), lambda i: (0, 0, 0))]
        + [pl.BlockSpec((block, 2 * width), lambda i, q=q: (i, q)) for q in range(parts)],
        out_specs=pl.BlockSpec((rows, block), lambda i: (0, i)),
        out_shape=jax.ShapeDtypeStruct((rows, units), F32),
        compiler_params=params(),
        name="grad_middle",
    )(cot_full, *[down_weight] * parts)


def spread_kernel(order, value_ref, weight_ref, *out_refs):
    result = jnp.dot(value_ref[...], weight_ref[...], preferred_element_type=F32).astype(BF16)
    for index, ref in enumerate(out_refs):

        @pl.when(lax.rem(pl.program_id(0), 4) == index)
        def _(ref=ref):
            ref[0] = result


def spread(order, value, weight, tokens):
    rows, units = value.shape
    width = weight.shape[1] // 8
    kernel, token_specs = ordered(spread_kernel, 3, tokens)
    return pl.pallas_call(
        kernel,
        grid_spec=pltpu.PrefetchScalarGridSpec(
            num_scalar_prefetch=1,
            grid=(8,),
            in_specs=[
                pl.BlockSpec((rows, units), lambda k, o: (0, 0)),
                pl.BlockSpec((units, width), lambda k, o: (0, o[k])),
            ]
            + token_specs,
            out_specs=[pl.BlockSpec((1, rows, width), lambda k, o: (k // 4, 0, 0))] * 4,
        ),
        out_shape=[jax.ShapeDtypeStruct((2, rows, width), BF16)] * 4,
        compiler_params=params(),
        name="ffn_out",
    )(order, value, weight, *tokens)


def kernel_grad_kernel(*refs):
    terms = refs[:5]
    cot_ref, hidden_ref, low_ref, high_ref, tap_ref = refs[5:10]
    grad_ref, logit_ref, padded, found_ref = refs[10:]
    rows, width = hidden_ref.shape
    heads = 2
    head_width = width // heads
    padded[0:PAD] = low_ref[...].astype(F32)
    padded[PAD : PAD + rows] = hidden_ref[...].astype(F32)
    padded[PAD + rows :] = high_ref[...].astype(F32)
    step = 32
    lane = lax.broadcasted_iota(jnp.int32, (step, ROWS), 1)

    def run(index, carry):
        base = pl.multiple_of(index * step, step)
        at = pl.ds(base, step)
        grad = terms[0][at, :].astype(F32)
        for ref in terms[1:]:
            grad = grad + ref[at, :].astype(F32)
        grad = grad + cot_ref[at, :].astype(F32)
        grad_ref[at, :] = grad
        taps = tap_ref[at, :]
        found = jnp.zeros((step, ROWS), F32)
        for head in range(heads):
            lanes = slice(head * head_width, (head + 1) * head_width)
            window = padded[pl.ds(base, step + 2 * PAD), lanes]
            part = grad[:, lanes]
            for tap in range(KW):
                column = head * KW + tap
                value = jnp.sum(part * window[tap + 1 : tap + 1 + step], axis=1, keepdims=True)
                found = jnp.where(lane == column, value, found)
        product = taps * found
        in_first = lane < KW
        one = jnp.sum(jnp.where(in_first, product, 0.0), axis=1, keepdims=True)
        two = jnp.sum(jnp.where(in_first, 0.0, product), axis=1, keepdims=True)
        found_ref[at, :] = taps * (found - jnp.where(in_first, one, two))
        return carry

    lax.fori_loop(0, rows // step, run, 0)
    logit_ref[...] = found_ref[...].T.astype(BF16)


def kernel_grads(pairs, last, cotangent, hidden, low, high, taps, tokens):
    rows, width = hidden.shape
    flat = pl.BlockSpec((rows, width), lambda i: (0, 0))
    edge = pl.BlockSpec((PAD, width), lambda i: (0, 0))
    kernel, token_specs = ordered(kernel_grad_kernel, 10, tokens)
    return pl.pallas_call(
        kernel,
        grid=(1,),
        in_specs=[pl.BlockSpec((None, rows, width), lambda i: (0, 0, 0))] * 4
        + [flat, flat, flat, edge, edge, pl.BlockSpec((rows, ROWS), lambda i: (0, 0))]
        + token_specs,
        out_specs=[flat, pl.BlockSpec((ROWS, rows), lambda i: (0, 0))],
        out_shape=(
            jax.ShapeDtypeStruct((rows, width), F32),
            jax.ShapeDtypeStruct((ROWS, rows), BF16),
        ),
        scratch_shapes=[
            pltpu.VMEM((rows + 2 * PAD, width), F32),
            pltpu.VMEM((rows, ROWS), F32),
        ],
        compiler_params=params(24),
        name="kernel_grads",
    )(*pairs, last, cotangent, hidden, low, high, taps, *tokens)


def hidden_grad_kernel(
    grad_ref,
    glow_ref,
    ghigh_ref,
    tap_ref,
    tlow_ref,
    thigh_ref,
    logit_ref,
    gen_ref,
    mask_ref,
    code_ref,
    embed_ref,
    table_ref,
    padded,
    tapped,
    back,
):
    rows, width = grad_ref.shape
    heads = 2
    head_width = width // heads
    padded[0:PAD] = glow_ref[...].astype(F32)
    padded[PAD : PAD + rows] = grad_ref[...]
    padded[PAD + rows :] = ghigh_ref[...].astype(F32)
    tapped[0:PAD] = tlow_ref[...]
    tapped[PAD : PAD + rows] = tap_ref[...]
    tapped[PAD + rows :] = thigh_ref[...]
    back[...] = lax.dot_general(logit_ref[...], gen_ref[...], TN, preferred_element_type=F32)
    step = 32

    def run(index, carry):
        base = pl.multiple_of(index * step, step)
        at = pl.ds(base, step)
        picked = mask_ref[at, :] == 1
        taps = tapped[pl.ds(base, step + 2 * PAD), :]
        for head in range(heads):
            lanes = slice(head * head_width, (head + 1) * head_width)
            window = padded[pl.ds(base, step + 2 * PAD), lanes]
            total = window[PAD : PAD + step] + back[at, lanes]
            for tap in range(KW):
                column = head * KW + tap
                lower = 2 * PAD - 1 - tap
                total = (
                    total
                    + taps[lower : lower + step, column : column + 1]
                    * window[lower : lower + step]
                )
            embed_ref[at, lanes] = jnp.where(picked, 0.0, total)
            back[at, lanes] = jnp.where(picked, total, 0.0)
        return carry

    lax.fori_loop(0, rows // step, run, 0)
    codes = lax.broadcasted_iota(jnp.int32, (table_ref.shape[0], rows), 0)
    chosen = jnp.where(codes == code_ref[...], 1.0, 0.0).astype(BF16)
    value = back[...]
    upper = value.astype(BF16)
    lower = (value - upper.astype(F32)).astype(BF16)
    table_ref[...] = jnp.dot(chosen, upper, preferred_element_type=F32) + jnp.dot(
        chosen, lower, preferred_element_type=F32
    )


def hidden_grads(operands, codes, tokens):
    rows, width = operands[0].shape
    kernel, token_specs = ordered(hidden_grad_kernel, len(operands), tokens)
    whole = [pl.BlockSpec(o.shape, lambda i: (0, 0)) for o in operands]
    return pl.pallas_call(
        kernel,
        grid=(1,),
        in_specs=whole + token_specs,
        out_specs=[
            pl.BlockSpec((rows, width), lambda i: (0, 0)),
            pl.BlockSpec((codes, width), lambda i: (0, 0)),
        ],
        out_shape=(
            jax.ShapeDtypeStruct((rows, width), F32),
            jax.ShapeDtypeStruct((codes, width), F32),
        ),
        scratch_shapes=[
            pltpu.VMEM((rows + 2 * PAD, width), F32),
            pltpu.VMEM((rows + 2 * PAD, ROWS), F32),
            pltpu.VMEM((rows, width), F32),
        ],
        compiler_params=params(24),
        name="hidden_grads",
    )(*operands, *tokens)


def gen_blocks_kernel(order, gen_ref, token_ref, out_ref):
    columns = gen_ref.shape[0]
    members, _, width = out_ref.shape
    out_ref[...] = jnp.zeros_like(out_ref)
    for k in range(members):
        at = pl.multiple_of(order[k] * width, width)
        out_ref[k, 0:columns] = gen_ref[:, pl.ds(at, width)]


def gen_blocks(order, gen_rows, width, token):
    columns, depth = gen_rows.shape
    members = depth // width
    return pl.pallas_call(
        gen_blocks_kernel,
        grid_spec=pltpu.PrefetchScalarGridSpec(
            num_scalar_prefetch=1,
            grid=(1,),
            in_specs=[
                pl.BlockSpec((columns, depth), lambda i, o: (0, 0)),
                pl.BlockSpec(memory_space=pltpu.HBM),
            ],
            out_specs=pl.BlockSpec((members, ROWS, width), lambda i, o: (0, 0, 0)),
        ),
        out_shape=jax.ShapeDtypeStruct((members, ROWS, width), BF16),
        compiler_params=params(24),
        name="gen_blocks",
    )(order, gen_rows, token)


def gen_grads_kernel(logit_ref, hidden_ref, out_ref):
    width = hidden_ref.shape[2]
    for piece in range(hidden_ref.shape[0]):
        out_ref[:, piece * width : (piece + 1) * width] = jnp.dot(
            logit_ref[...], hidden_ref[piece], preferred_element_type=F32
        )


def gen_grads(logit_grad, hidden_full):
    members, rows, width = hidden_full.shape
    heads = logit_grad.shape[0]
    return pl.pallas_call(
        gen_grads_kernel,
        out_shape=jax.ShapeDtypeStruct((heads, members * width), F32),
        compiler_params=params(24),
        name="gen_grads",
    )(logit_grad, hidden_full)


def add_up(values):
    total = values[0].astype(F32)
    for value in values[1:]:
        total = total + value.astype(F32)
    return total


def swap_pairs(pairs):
    return [pairs[0]] + [flip(pairs[z], "tp", z) for z in (1, 2, 3)]


def body(
    embeddings,
    span_mask,
    sentinel_id,
    sentinel_table,
    gen_weight,
    up_weight,
    down_weight,
    cotangent,
):
    rows, width = embeddings.shape
    codes = sentinel_table.shape[0]
    members = lax.axis_size("tp")
    me = lax.axis_index("tp")
    order = jnp.arange(members, dtype=jnp.int32) ^ me.astype(jnp.int32)

    sentinel_codes = jnp.arange(codes, dtype=jnp.int32)
    onehot = (sentinel_id[:, None] == sentinel_codes[None, :]).astype(BF16)
    picked = jnp.dot(onehot, sentinel_table, preferred_element_type=F32).astype(BF16)
    hidden = jnp.where(span_mask[:, None] == 1, picked, embeddings)
    pieces = gather_pieces(hidden)
    cot_full = lax.all_gather(cotangent, "tp", axis=0, tiled=False)

    hidden_full, edges, flat, taps = hidden_logits(order, pieces, gen_weight.T)
    high_full, low_full = edges[0], edges[1]
    count = lax.axis_size("seq")
    low_full = lax.ppermute(low_full, "seq", [(i, i + 1) for i in range(count - 1)])
    high_full = lax.ppermute(high_full, "seq", [(i + 1, i) for i in range(count - 1)])
    middle_grad = grad_middle(cot_full, down_weight)
    flat_full = gather_small(flat, (middle_grad,))

    columns = gen_weight.shape[1]
    gen_full = gen_blocks(order, gen_weight.T, width, hidden_full)
    gen_full = exchange(gen_full, (1, 2))

    summed, act, middle, *back_own = layer(
        order,
        hidden_full,
        low_full,
        high_full,
        flat_full,
        up_weight,
        middle_grad,
        cot_full,
        (gen_full,),
    )
    back_pairs = swap_pairs(back_own)
    summed = lax.psum_scatter(summed, "seq", scatter_dimension=0, tiled=False)
    gen_full = exchange(gen_full, (4,))
    tap_low, tap_high = halo(taps)
    out_own = spread(order, middle, down_weight, (gen_full, tap_low, tap_high))
    out_pairs = swap_pairs(out_own)
    gen_full = gen_full.reshape(members * ROWS, width)

    out_last = flip(add_up([pair[1] for pair in out_pairs]).astype(BF16), "tp", 4)
    back_last = flip(add_up([pair[1] for pair in back_pairs]).astype(BF16), "tp", 4)
    low = lax.dynamic_index_in_dim(low_full, me, 0, keepdims=False)
    high = lax.dynamic_index_in_dim(high_full, me, 0, keepdims=False)
    grad, logit_grad = kernel_grads(
        back_pairs,
        back_last,
        cotangent,
        hidden,
        low,
        high,
        taps,
        (gen_full, tap_low, tap_high, out_own[0]),
    )
    grad_low, grad_high = halo(grad.astype(BF16))
    logit_full = gather_far_first(logit_grad).reshape(members * ROWS, rows)
    gen_sum = sum_over_seq(gen_grads(logit_grad, hidden_full), (1, 2))
    embed_grad, table_part = hidden_grads(
        (
            grad,
            grad_low,
            grad_high,
            taps,
            tap_low,
            tap_high,
            logit_full,
            gen_full,
            span_mask[:, None],
            sentinel_id[None, :],
        ),
        codes,
        (gen_sum, out_last),
    )
    gen_sum = sum_over_seq(gen_sum, (8, 4))
    gen_grad = gen_sum[:columns].T
    table_grad = sum_over_seq(table_part)

    total = add_up([pair[0] for pair in out_pairs] + [out_last])
    layer_output = (act.astype(F32) + total).astype(BF16)

    chunk = summed.shape[0] // 2
    up_grad = summed[:chunk].astype(F32)
    down_grad = summed[chunk:].astype(F32).T
    return (layer_output, embed_grad, table_grad, gen_grad, up_grad, down_grad)


def solution(mesh):
    placed = (
        P("seq", "tp"),
        P("seq"),
        P("seq"),
        P(None, "tp"),
        P(None, "tp"),
        P(None, "tp"),
        P("tp", None),
        P("seq", "tp"),
    )
    return jax.shard_map(
        body,
        mesh=mesh,
        in_specs=placed,
        out_specs=(
            P("seq", "tp"),
            P("seq", "tp"),
            P(None, "tp"),
            P(None, "tp"),
            P("seq", "tp"),
            P("tp", "seq"),
        ),
        check_vma=False,
    )
```
